256 devices in a mesh: ctx: 8 (over z), head: 32 (over y, x, core).
Axes of the slice: x: 4, y: 4, z: 8, core: 2. Of those that a mesh axis runs over, the one named last changes fastest.
Arguments:
- x_stream: bfloat16 [32768, 16384], P('ctx', 'head'), may hold values from -6 to 6
- gate_z: bfloat16 [32768, 16384], P('ctx', 'head'), as said below
- state_proj: bfloat16 [32768, 2048], P('ctx', 'head'), may hold values from -5 to 5
- dt_raw: float32 [32768, 256], P('ctx', 'head'), as said below
- dt_bias: float32 [256], P('head'), may hold values from -3 to -1
- a_log: float32 [256], P('head'), as said below
- skip_d: float32 [256], P('head'), may hold values from 0.5 to 1.5
- conv_x: bfloat16 [4, 16384], P(None, 'head'), may hold values from -3 to 3
- conv_proj: bfloat16 [4, 2048], P(None, 'head'), may hold values from -3 to 3
- norm_gain: float32 [16384], P('head'), may hold values from 0.5 to 1.5
Outputs:
- mixer_out: bfloat16 [32768, 16384], P('ctx', 'head')
The draws below stay inside these ranges and needn't reach their ends.
Inputs may be any that keep to these rules, and one draw needn't show every extreme that they name: gate_z is a bounded normal draw whose scale varies by column. dt_raw is bounded; its level varies over blocks of 4096 tokens and heads. a_log is finite.
All inputs are finite; a program needn't handle non-finite values.
Results may differ from the reference program's by a relative error of at most 0.0085.
Values may be sent and summed in bfloat16 or wider, within the bound.
No kernel may reach another device: no remote copies, remote signals or barrier semaphores. Data moves between devices by JAX's collectives and lax.ppermute only.
A program may use at most 128 MiB of HBM per device.

```python
import math
import jax
import jax.numpy as jnp
from jax import lax

HEADS = 256
HEADDIM = 64
STATE = 128
GROUPS = 8
KCONV = 4
BLOCK_LEN = 128
TOK_DEV = 4096
TOKENS = 32768


def draw_gate_z(key, part):
    per_group = HEADS // GROUPS
    column = (jnp.arange(HEADS * HEADDIM) // HEADDIM % per_group).astype(jnp.float32)
    noise_part = jax.random.truncated_normal(key, -5.0, 5.0, (TOKENS, HEADS * HEADDIM), jnp.float32)
    rising = 0.5 + column / (per_group - 1.0)
    col_scale = rising
    return (noise_part * col_scale).astype(jnp.bfloat16)


def draw_dt_raw(key, part):
    blocks = TOKENS // TOK_DEV
    levels = jax.random.uniform(jax.random.fold_in(key, 11), (blocks, HEADS), jnp.float32, -0.7, 0.7)
    noise_part = 0.5 * jax.random.truncated_normal(key, -4.0, 4.0, (TOKENS, HEADS), jnp.float32)
    return noise_part + jnp.repeat(levels, TOK_DEV, axis=0)


def draw_a_log(key, part):
    typical_step = 0.127
    slow_rate = jnp.exp(jax.random.uniform(jax.random.fold_in(key, 3), (HEADS,), jnp.float32, math.log(0.3), math.log(2.0))) / TOKENS
    fast_rate = jnp.exp(jax.random.uniform(jax.random.fold_in(key, 5), (HEADS,), jnp.float32, math.log(0.02), math.log(0.06)))
    share = 0.5
    slow_mask = jax.random.uniform(jax.random.fold_in(key, 9), (HEADS,), jnp.float32) < share
    rate_per_token = jnp.where(slow_mask, slow_rate, fast_rate)
    return jnp.log(rate_per_token / typical_step)


def steps_of(key, extent, shards, smallest, high):
    factor_of, own = 1.0, jax.random.fold_in(key, 6)
    for axis_at, parts in shards:
        steps = jnp.exp(jax.random.uniform(jax.random.fold_in(own, axis_at), (parts,), jnp.float32, smallest / len(shards), high / len(shards)))
        factor_of = factor_of * jnp.repeat(steps, extent[axis_at] // parts).reshape([-1 if axis == axis_at else 1 for axis in range(len(extent))])
    return factor_of


def noise(stream_key, dims, deviation, reach, pieces=(), kind=jnp.bfloat16):
    array = jax.random.normal(stream_key, dims, jnp.float32) * deviation
    if len(pieces) > 0:
        array = steps_of(stream_key, dims, pieces, -0.22, 0.18) * array
    return jnp.clip(array, min=-reach, max=reach).astype(kind)


def setup_inputs(seed: int = 0) -> dict:
    keys = jax.random.split(jax.random.key(seed), 11)
    return {
        "x_stream": noise(keys[0], (TOKENS, HEADS * HEADDIM), 1.0, 6.0, ((0, 8), (1, 32))),
        "gate_z": draw_gate_z(jax.random.fold_in(keys[10], 71), 0),
        "state_proj": noise(keys[2], (TOKENS, 2 * GROUPS * STATE), 0.35, 5.0, ((0, 8), (1, 32))),
        "dt_raw": draw_dt_raw(jax.random.fold_in(keys[10], 71), 0),
        "dt_bias": jnp.clip(-3.0 + 2.0 * jax.random.uniform(keys[4], (HEADS,), jnp.float32) ** steps_of(keys[4], (HEADS,), ((0, 32),), -0.2, 0.2), -3.0, -1.0),
        "a_log": draw_a_log(jax.random.fold_in(keys[10], 71), 0),
        "skip_d": jnp.clip(0.5 + 1.0 * jax.random.uniform(keys[6], (HEADS,), jnp.float32) ** steps_of(keys[6], (HEADS,), ((0, 32),), -0.2, 0.2), 0.5, 1.5),
        "conv_x": noise(keys[7], (KCONV, HEADS * HEADDIM), KCONV ** -0.5, 3.0, ((1, 32),)),
        "conv_proj": noise(keys[8], (KCONV, 2 * GROUPS * STATE), KCONV ** -0.5, 3.0, ((1, 32),)),
        "norm_gain": jnp.clip(1.0 + 0.1 * jax.random.normal(keys[9], (HEADS * HEADDIM,), jnp.float32), 0.5, 1.5),
    }


def conv_silu(sequence, edge_rows, weight):
    kernel_len = weight.shape[0]
    length = sequence.shape[0]
    padded = jnp.concatenate([edge_rows, sequence], axis=0).astype(jnp.float32)
    weight_wide = weight.astype(jnp.float32)
    total = jnp.zeros(sequence.shape, jnp.float32)
    for offset in range(kernel_len):
        total = total + weight_wide[offset] * padded[offset:offset + length]
    return jax.nn.silu(total).astype(jnp.bfloat16)

def block_scan(x_blocks, b_blocks, c_blocks, step_size, log_decay, initial):
    highest = lax.Precision.HIGHEST
    running = jnp.cumsum(jnp.swapaxes(log_decay, 1, 2), axis=2)
    step_heads = jnp.swapaxes(step_size, 1, 2)
    b_wide = b_blocks.astype(jnp.float32)
    c_wide = c_blocks.astype(jnp.float32)
    x_wide = x_blocks.astype(jnp.float32)
    gram_matrix = jnp.einsum('ctn,csn->cts', c_wide, b_wide, precision=highest)
    block_len = running.shape[2]
    row_ids = jnp.arange(block_len)[:, None]
    col_ids = jnp.arange(block_len)[None, :]
    causal_mask = row_ids >= col_ids
    log_gaps = running[:, :, :, None] - running[:, :, None, :]
    decay_matrix = jnp.where(causal_mask, jnp.exp(jnp.where(causal_mask, log_gaps, 0.0)), 0.0)
    weights = (gram_matrix[:, None] * decay_matrix * step_heads[:, :, None, :]).astype(jnp.bfloat16)
    intra_out = jnp.einsum('chts,cshp->cthp', weights.astype(jnp.float32), x_wide, precision=highest)
    block_total = running[:, :, -1]
    state_weight = jnp.exp(block_total[:, :, None] - running) * step_heads
    weighted = (x_wide * jnp.swapaxes(state_weight, 1, 2)[..., None]).astype(jnp.bfloat16)
    states = jnp.einsum('cshp,csn->chpn', weighted.astype(jnp.float32), b_wide, precision=highest)

    def advance(state_now, inputs):
        factor, addend = inputs
        return (factor[:, None, None] * state_now + addend, state_now)
    final_state, entering = lax.scan(advance, initial, (jnp.exp(block_total), states))
    inter_out = jnp.exp(jnp.swapaxes(running, 1, 2))[..., None] * jnp.einsum('ctn,chpn->cthp', c_wide, entering, precision=highest)
    return (intra_out + inter_out, final_state, block_total, running)

def reference(x_stream, gate_z, state_proj, dt_raw, dt_bias, a_log, skip_d, conv_x, conv_proj, norm_gain):
    kernel_len = conv_x.shape[0]
    proj_conv = conv_silu(state_proj, jnp.zeros((kernel_len - 1, state_proj.shape[1]), jnp.bfloat16), conv_proj)
    step_size = jax.nn.softplus(dt_raw + dt_bias)
    log_decay = step_size * -jnp.exp(a_log)
    per_group = HEADS // GROUPS
    blocks = TOKENS // BLOCK_LEN
    gains = norm_gain.reshape(HEADS, HEADDIM)

    def group_out(group_id):
        own_cols = lax.dynamic_slice_in_dim(proj_conv, group_id * 2 * STATE, 2 * STATE, 1)
        b_blocks = own_cols[:, :STATE].reshape(blocks, BLOCK_LEN, STATE)
        c_blocks = own_cols[:, STATE:].reshape(blocks, BLOCK_LEN, STATE)

        def head_out(head_local):
            head_id = group_id * per_group + head_local
            x_head = lax.dynamic_slice_in_dim(x_stream, head_id * HEADDIM, HEADDIM, 1)
            w_head = lax.dynamic_slice_in_dim(conv_x, head_id * HEADDIM, HEADDIM, 1)
            x_conv = conv_silu(x_head, jnp.zeros((kernel_len - 1, HEADDIM), jnp.bfloat16), w_head)
            step_head = lax.dynamic_slice_in_dim(step_size, head_id, 1, 1).reshape(blocks, BLOCK_LEN, 1)
            decay_head = lax.dynamic_slice_in_dim(log_decay, head_id, 1, 1).reshape(blocks, BLOCK_LEN, 1)
            mixed, final_state, block_total, running = block_scan(x_conv.reshape(blocks, BLOCK_LEN, 1, HEADDIM), b_blocks, c_blocks, step_head, decay_head, jnp.zeros((1, HEADDIM, STATE), jnp.float32))
            skip_head = lax.dynamic_slice_in_dim(skip_d, head_id, 1, 0)
            mixed = mixed.reshape(TOKENS, HEADDIM) + skip_head * x_conv.astype(jnp.float32)
            z_head = lax.dynamic_slice_in_dim(gate_z, head_id * HEADDIM, HEADDIM, 1).astype(jnp.float32)
            return mixed * jax.nn.silu(z_head)
        gated_out = lax.map(head_out, jnp.arange(per_group, dtype=jnp.int32))
        mean_square = lax.optimization_barrier(jnp.mean(gated_out * gated_out, axis=(0, 2)))
        gain_group = lax.dynamic_slice_in_dim(gains, group_id * per_group, per_group, 0)
        normed = gated_out * lax.rsqrt(mean_square + 1e-05)[None, :, None] * gain_group[:, None, :]
        return normed.astype(jnp.bfloat16)
    normed = lax.map(group_out, jnp.arange(GROUPS, dtype=jnp.int32))
    return jnp.transpose(normed, (2, 0, 1, 3)).reshape(TOKENS, HEADS * HEADDIM)
```

```python
import jax
import jax.numpy as jnp
from jax import lax
from jax.experimental import pallas as pl
from jax.experimental.pallas import tpu as pltpu
from jax.sharding import PartitionSpec as P

HEADS = 256
STATE = 128
GROUPS = 8
BLK = 128
LOG2E = 1.4426950408889634
F32 = jnp.float32
BF16 = jnp.bfloat16
HIGH = lax.Precision.HIGHEST
VMEM_CAP = 8 * 1024 * 1024
LOCAL_UNROLL = 8
CARRY_UNROLL = 8
CONV_UNROLL = (5, 8)
STATE_UNROLL = 8


def shifted(x, axis, by):
    count = lax.axis_size(axis)
    pairs = [(i, i + by) for i in range(count) if 0 <= i + by < count]
    return lax.ppermute(x, axis, pairs)


def rotated(x, axis, by):
    count = lax.axis_size(axis)
    return lax.ppermute(x, axis, [(i, (i + by) % count) for i in range(count)])


def swapped(value, axis, mask):
    return lax.ppermute(value, axis, [(i, i ^ mask) for i in range(lax.axis_size(axis))])


def after(value, *others):
    return lax.optimization_barrier((value,) + others)[0]


def params():
    return pltpu.CompilerParams(vmem_limit_bytes=VMEM_CAP)


def cost(flops, size, trans=0):
    return pl.CostEstimate(flops=flops, bytes_accessed=size, transcendentals=trans)


def specs(count, scalars=0):
    smem = pl.BlockSpec(memory_space=pltpu.SMEM)
    return [smem] * scalars + [pl.BlockSpec(memory_space=pltpu.VMEM)] * (count - scalars)


def half_silu(h):
    return h + h * jnp.tanh(h)


def iota(shape, dim):
    return lax.broadcasted_iota(jnp.int32, shape, dim)


def block_at(i):
    return pl.ds(pl.multiple_of(i * BLK, BLK), BLK)


def head_spread(heads, chans):
    return (iota((heads, chans), 1) // (chans // heads) == iota((heads, chans), 0)).astype(BF16)


def upright(row):
    count = row.shape[1]
    eye = iota((count, count), 0) == iota((count, count), 1)
    return jnp.sum(jnp.where(eye, row, 0.0), axis=1, keepdims=True)


def tails_kernel(x_ref, p_ref, w_ref, o_ref):
    half, chans = p_ref.shape[0], x_ref.shape[1]
    o_ref[0:half, :] = p_ref[...]
    for at in range(chans // BLK):
        lo = half + 16 * at
        o_ref[lo : lo + 16, :] = x_ref[:, at * BLK : (at + 1) * BLK]
    at = half + 16 * (chans // BLK)
    o_ref[at : at + 16, :] = jnp.zeros((16, BLK), BF16)
    o_ref[at : at + 4, 0:half] = w_ref[...]


def tails(x, proj_t, taps):
    tokens, chans = x.shape
    half = proj_t.shape[0]
    rows = half + 16 * (chans // BLK) + 16
    return pl.pallas_call(
        tails_kernel,
        grid=(1,),
        in_specs=[
            pl.BlockSpec((16, chans), lambda i: (tokens // 16 - 1, 0)),
            pl.BlockSpec((half, BLK), lambda i: (0, tokens // BLK - 1)),
            pl.BlockSpec(taps.shape, lambda i: (0, 0)),
        ],
        out_specs=pl.BlockSpec((rows, BLK), lambda i: (0, 0)),
        out_shape=jax.ShapeDtypeStruct((rows, BLK), BF16),
        compiler_params=pltpu.CompilerParams(vmem_limit_bytes=60 * 1024 * 1024),
        name="tails",
    )(x, proj_t, taps)


def proj_conv_kernel(flag_ref, p_ref, halo_ref, o_ref):
    rows, tokens = p_ref.shape
    group = 16
    lane = iota((group, BLK), 1)
    at = halo_ref.shape[0] - 16
    weights = jnp.transpose(0.5 * halo_ref[at : at + 16, :].astype(F32)[0:8])
    for lo in range(0, rows, group):
        span = slice(lo, lo + group)
        taps = [jnp.broadcast_to(weights[span, k : k + 1], (group, BLK)) for k in range(4)]
        halo = jnp.where(flag_ref[1] == 0, 0.0, halo_ref[span, :].astype(F32))
        prev = [pltpu.roll(halo, k, 1) for k in (1, 2, 3)]
        for i in range(tokens // BLK):
            cur = p_ref[span, i * BLK : (i + 1) * BLK].astype(F32)
            now = [pltpu.roll(cur, k, 1) for k in (1, 2, 3)]
            h = taps[3] * cur
            for k in (1, 2, 3):
                h = h + taps[3 - k] * jnp.where(lane < k, prev[k - 1], now[k - 1])
            o_ref[span, i * BLK : (i + 1) * BLK] = half_silu(h).astype(BF16)
            prev = now


def proj_conv(flag, proj_t, halo):
    rows, tokens = proj_t.shape
    return pl.pallas_call(
        proj_conv_kernel,
        in_specs=specs(3, 1),
        out_specs=specs(1)[0],
        out_shape=jax.ShapeDtypeStruct((rows, tokens), BF16),
        compiler_params=params(),
        cost_estimate=cost(rows * tokens * 4000, rows * tokens * 4, rows * tokens),
        name="proj_conv",
    )(flag, proj_t, halo)


def decay_kernel(
    dt_ref, bias_ref, alog_ref, skip_ref, run_ref, abs_ref, step_ref, tot_ref, wide_ref
):
    heads, tokens = dt_ref.shape
    blocks = tokens // BLK
    chans = tot_ref.shape[1]
    raw = dt_ref[...] + upright(bias_ref[...])
    step = jnp.maximum(raw, 0.0) + jnp.log1p(jnp.exp(-jnp.abs(raw)))
    step_ref[...] = step
    log_decay = step * (-LOG2E * jnp.exp(upright(alog_ref[...])))
    stack = jnp.concatenate(
        [log_decay[:, b * BLK : (b + 1) * BLK] for b in range(blocks)], axis=0
    )
    upper = (iota((BLK, BLK), 0) <= iota((BLK, BLK), 1)).astype(F32)
    run = jnp.dot(stack, upper, precision=HIGH, preferred_element_type=F32)
    total = run[:, BLK - 1 : BLK]
    count = blocks * heads
    r, c = iota((count, count), 0), iota((count, count), 1)
    before = ((c // heads < r // heads) & (c % heads == r % heads)).astype(F32)
    start = jnp.dot(
        before,
        jnp.broadcast_to(total, (count, BLK)),
        precision=HIGH,
        preferred_element_type=F32,
    )
    whole = run + start
    for b in range(blocks):
        run_ref[:, b * BLK : (b + 1) * BLK] = run[b * heads : (b + 1) * heads]
        abs_ref[:, b * BLK : (b + 1) * BLK] = whole[b * heads : (b + 1) * heads]
    pick = (iota((blocks, count), 1) // heads == iota((blocks, count), 0)).astype(F32)
    chan_head = iota((count, chans), 1) // (chans // heads)
    spread = jnp.where(chan_head == iota((count, chans), 0) % heads, total, 0.0)
    own = iota((heads, chans), 1) // (chans // heads) == iota((heads, chans), 0)
    wide_ref[...] = jnp.sum(
        jnp.where(own, upright(skip_ref[...]), 0.0), axis=0, keepdims=True
    )
    tot_ref[...] = jnp.dot(pick, spread, precision=HIGH, preferred_element_type=F32)


def decays(dt_t, bias, a_log, skip, chans):
    heads, tokens = dt_t.shape
    rows = jax.ShapeDtypeStruct((heads, tokens), F32)
    return pl.pallas_call(
        decay_kernel,
        in_specs=specs(4),
        out_specs=tuple(specs(5)),
        out_shape=(
            rows,
            rows,
            rows,
            jax.ShapeDtypeStruct((tokens // BLK, chans), F32),
            jax.ShapeDtypeStruct((1, chans), F32),
        ),
        compiler_params=params(),
        cost_estimate=cost(heads * tokens * 20000, heads * tokens * 16, heads * tokens * 2),
        name="decays",
    )(dt_t, bias[None, :], a_log[None, :], skip[None, :])


def chan_conv_kernel(base, flag_ref, x_ref, w_ref, run_ref, step_ref, *rest):
    o_ref, v_ref, t_ref = rest[-3:]
    halo_ref = rest[0]
    chans = x_ref.shape[1]
    heads = run_ref.shape[0]
    count = o_ref.shape[0] // BLK
    spread = head_spread(heads, chans)

    def block(i, tails):
        src, dst = block_at(base + i), block_at(i)
        run = run_ref[:, src]
        coef = (jnp.exp2(run[:, BLK - 1 : BLK] - run) * step_ref[:, src]).astype(BF16)
        wide = lax.dot_general(
            coef, spread, (((0,), (0,)), ((), ())), preferred_element_type=F32
        )
        for at in range(chans // BLK):
            lanes = slice(at * BLK, (at + 1) * BLK)
            taps = [0.5 * w_ref[k : k + 1, lanes].astype(F32) for k in range(4)]
            cur = x_ref[src, lanes].astype(F32)
            ext = jnp.concatenate([tails(at).astype(F32)[8:16], cur], axis=0)
            back = pltpu.roll(ext, 1, 0)
            older = pltpu.roll(taps[1] * ext + taps[0] * back, 2, 0)
            y = half_silu(taps[3] * cur + taps[2] * back[8:] + older[8:])
            o_ref[dst, lanes] = y.astype(BF16)
            v_ref[dst, lanes] = (y * wide[:, lanes]).astype(BF16)

    def from_halo(at):
        lo = halo_ref.shape[0] - 16 - 16 * (chans // BLK) + 16 * at
        part = halo_ref[lo : lo + 16, :]
        return jnp.where(flag_ref[1] == 0, jnp.zeros_like(part), part)

    def inner(i):
        def tail(at):
            lo = pl.multiple_of((base + i) * BLK - 16, 16)
            return x_ref[pl.ds(lo, 16), at * BLK : (at + 1) * BLK]

        block(i, tail)

    first = 1 if base == 0 else 0
    if first:
        block(0, from_halo)

    @pl.loop(first, count, unroll=CONV_UNROLL[0] if first else CONV_UNROLL[1])
    def _(i):
        inner(i)

    t_ref[...] = jnp.zeros_like(t_ref)


def chan_conv(flag, x, taps, run, step, halo, part, parts):
    tokens, chans = x.shape
    here = tokens // parts

    def kernel(*refs):
        chan_conv_kernel(part * here // BLK, *refs)

    return pl.pallas_call(
        kernel,
        in_specs=specs(5 + (part == 0), 1),
        out_specs=tuple(specs(3)),
        out_shape=(jax.ShapeDtypeStruct((here, chans), BF16),) * 2
        + (jax.ShapeDtypeStruct((8, BLK), F32),),
        compiler_params=params(),
        cost_estimate=cost(here * chans * 4000, here * chans * 6, here * chans),
        name="chan_conv",
    )(flag, x, taps, run, step, *([halo] if part == 0 else []))


def pick_quarters(flag_ref, quarter_refs, at):
    own, near, far, cross = (ref[:, at] for ref in quarter_refs)
    here = jnp.concatenate([own, near], axis=0)
    there = jnp.concatenate([far, cross], axis=0)
    return here, there, flag_ref[0] == 0


def state_kernel(flag_ref, own_ref, near_ref, far_ref, cross_ref, tot_ref, *rest):
    s_ref, msg_ref, now_ref = rest[-3:]
    v_refs = rest[:-3]
    chans = s_ref.shape[2]
    now_ref[...] = jnp.zeros_like(now_ref)
    for at, v_ref in enumerate(v_refs):
        count = v_ref.shape[0] // BLK
        base = at * count

        @pl.loop(0, count, unroll=STATE_UNROLL)
        def _(i):
            here, there, local_b = pick_quarters(
                flag_ref, (own_ref, near_ref, far_ref, cross_ref), block_at(base + i)
            )
            b = jnp.where(local_b, here, there)
            add = jnp.dot(b, v_ref[block_at(i), :], preferred_element_type=F32)
            now = now_ref[...]
            s_ref[base + i] = now.astype(BF16)
            now_ref[...] = jnp.exp2(tot_ref[pl.ds(base + i, 1), :]) * now + add

    log = jnp.sum(tot_ref[...], axis=0, keepdims=True)
    high = log.astype(BF16).astype(F32)
    mid = (log - high).astype(BF16).astype(F32)
    low = (log - high) - mid
    row = iota((16, chans), 0)
    parts = jnp.where(row == 0, high, jnp.where(row == 1, mid, jnp.where(row == 2, low, 0.0)))
    msg_ref[0:STATE, :] = now_ref[...].astype(BF16)
    msg_ref[STATE : STATE + 16, :] = parts.astype(BF16)


def states(flag, weighted, quarters, totals):
    blocks, chans = totals.shape
    return pl.pallas_call(
        state_kernel,
        in_specs=specs(6 + len(weighted), 1),
        out_specs=tuple(specs(2)),
        out_shape=(
            jax.ShapeDtypeStruct((blocks, STATE, chans), BF16),
            jax.ShapeDtypeStruct((STATE + 16, chans), BF16),
        ),
        scratch_shapes=[pltpu.VMEM((STATE, chans), F32)],
        compiler_params=params(),
        cost_estimate=cost(blocks * BLK * chans * 2000, blocks * BLK * chans * 4),
        name="states",
    )(flag, *quarters, totals, *weighted)


def local_kernel(
    base, offset, flag_ref, x_ref, own_ref, near_ref, far_ref, cross_ref, s_ref, run_ref, step_ref,
    skip_ref, o_ref
):
    tokens, chans = o_ref.shape
    heads = run_ref.shape[0]
    causal = iota((BLK, BLK), 0) >= iota((BLK, BLK), 1)
    left = iota((2 * BLK, BLK), 1) < chans // heads

    @pl.loop(0, tokens // BLK, unroll=LOCAL_UNROLL)
    def _(i):
        at = block_at(base + i)
        here, there, local_b = pick_quarters(
            flag_ref, (own_ref, near_ref, far_ref, cross_ref), at
        )
        c = jnp.transpose(jnp.where(local_b, there, here))
        b = jnp.where(local_b, here, there)
        gram = jnp.dot(c, b, preferred_element_type=F32)
        gram = jnp.where(causal, gram, 0.0).astype(BF16)
        run = run_ref[:, at]
        run_t = jnp.transpose(run)
        step = step_ref[:, at].astype(BF16)
        for pair in range(heads // 2):
            lanes = slice(pair * BLK, (pair + 1) * BLK)
            mats = []
            for h in (2 * pair, 2 * pair + 1):
                column = jnp.broadcast_to(run_t[:, h : h + 1], (BLK, BLK))
                gap = (column - run[h : h + 1, :]).astype(BF16)
                mats.append(jnp.exp2(jnp.minimum(gap, 0.0)) * gram * step[h : h + 1, :])
                mats.append(jnp.exp2(column.astype(BF16)) * c)
            lhs = jnp.concatenate(mats, axis=1)
            xs = x_ref[block_at(offset + i), lanes]
            both = jnp.concatenate([xs, s_ref[base + i, :, lanes]], axis=0)
            zero = jnp.zeros_like(both)
            rhs = jnp.concatenate(
                [jnp.where(left, both, zero), jnp.where(left, zero, both)], axis=0
            )
            out = jnp.dot(lhs, rhs, preferred_element_type=F32)
            out = out + skip_ref[:, lanes] * xs.astype(F32)
            o_ref[block_at(i), lanes] = out.astype(BF16)


def local(flag, x_conv, quarters, entering, run, step, skip, part, parts, offset):
    heads, tokens = run.shape
    chans = x_conv.shape[1]
    here = tokens // parts

    def kernel(*refs):
        local_kernel(part * here // BLK, offset, *refs)

    return pl.pallas_call(
        kernel,
        in_specs=specs(10, 1),
        out_specs=specs(1)[0],
        out_shape=jax.ShapeDtypeStruct((here, chans), BF16),
        compiler_params=params(),
        cost_estimate=cost(8000 * here * chans, here * chans * 6, here * heads * BLK * 2),
        name="local",
    )(flag, x_conv, *quarters, entering, run, step, skip)


def carry_kernel(nloc, flag_ref, own_ref, near_ref, far_ref, cross_ref, abs_ref, z_ref, *rest):
    l_refs, msgs = rest[:nloc], rest[nloc:-4]
    g_ref, q_ref, s_ref, acc_ref = rest[-4:]
    chans = g_ref.shape[1]
    heads = abs_ref.shape[0]
    gone = jnp.zeros((1, chans), F32)
    for d, msg in enumerate(msgs, 1):
        factor = jnp.where(flag_ref[1] >= d, jnp.exp2(gone), 0.0)
        term = factor * msg[0:STATE, :].astype(F32)
        acc_ref[...] = term if d == 1 else acc_ref[...] + term
        parts = msg[STATE : STATE + 16, :].astype(F32)
        gone = gone + ((parts[0:1] + parts[1:2]) + parts[2:3])
    s_ref[...] = acc_ref[...].astype(BF16)
    spread = head_spread(heads, chans)
    done = 0
    for l_ref in l_refs:
        count = l_ref.shape[0] // BLK
        first = done
        done += count

        @pl.loop(0, count, unroll=CARRY_UNROLL)
        def _(i):
            at = block_at(first + i)
            here, there, local_b = pick_quarters(
                flag_ref, (own_ref, near_ref, far_ref, cross_ref), at
            )
            c = jnp.transpose(jnp.where(local_b, there, here))
            wide = lax.dot_general(
                jnp.exp2(abs_ref[:, at]).astype(BF16),
                spread,
                (((0,), (0,)), ((), ())),
                preferred_element_type=F32,
            )
            carried = jnp.dot(c, s_ref[...], preferred_element_type=F32)
            folded = None
            for lo in range(0, chans, BLK):
                lanes = slice(lo, lo + BLK)
                gated = l_ref[block_at(i), lanes].astype(F32) + wide[:, lanes] * carried[:, lanes]
                gated = gated * half_silu(0.5 * z_ref[at, lanes].astype(F32))
                g_ref[at, lanes] = gated.astype(BF16)
                square = gated * gated
                folded = square if folded is None else folded + square
            q_ref[pl.ds(first + i, 1), :] = jnp.sum(jnp.transpose(folded), axis=0, keepdims=True)


def carry(flag, locs, gate, quarters, whole, msgs):
    heads, tokens = whole.shape
    chans = locs[0].shape[1]

    def kernel(*refs):
        carry_kernel(len(locs), *refs)

    return pl.pallas_call(
        kernel,
        in_specs=specs(7 + len(locs) + len(msgs), 1),
        out_specs=tuple(specs(2)),
        scratch_shapes=[pltpu.VMEM((STATE, chans), BF16), pltpu.VMEM((STATE, chans), F32)],
        out_shape=(
            jax.ShapeDtypeStruct((tokens, chans), BF16),
            jax.ShapeDtypeStruct((tokens // BLK, BLK), F32),
        ),
        compiler_params=params(),
        cost_estimate=cost(4000 * tokens * chans, tokens * chans * 6, tokens * chans),
        name="carry",
    )(flag, *quarters, whole, gate, *locs, *msgs)


def norm_kernel(width, g_ref, q_ref, gain_ref, o_ref):
    tokens, chans = o_ref.shape
    per = tokens // BLK
    first = pl.program_id(0) * per
    for i in range(per):
        at = slice(i * BLK, (i + 1) * BLK)
        scale = lax.rsqrt(q_ref[pl.ds(first + i, 1), :] * (1.0 / width) + 1e-05)
        column = jnp.transpose(jnp.broadcast_to(scale, (BLK, BLK)))
        for lo in range(0, chans, BLK):
            lanes = slice(lo, lo + BLK)
            g = g_ref[block_at(first + i), lanes].astype(F32)
            o_ref[at, lanes] = (g * column * gain_ref[:, lanes]).astype(BF16)


def norm(gated, squares, gain, width, rows=1024):
    tokens, chans = gated.shape

    def kernel(*refs):
        norm_kernel(width, *refs)

    return pl.pallas_call(
        kernel,
        grid=(tokens // rows,),
        in_specs=specs(3),
        out_specs=pl.BlockSpec((rows, chans), lambda i: (i, 0)),
        out_shape=jax.ShapeDtypeStruct((tokens, chans), BF16),
        compiler_params=params(),
        cost_estimate=cost(tokens * chans * 3, tokens * chans * 4),
        name="norm",
    )(gated, squares, gain)


def on_device(
    x_stream, gate_z, state_proj, dt_raw, dt_bias, a_log, skip_d, conv_x, conv_proj, norm_gain
):
    tokens, chans = x_stream.shape
    heads = dt_raw.shape[1]
    head_pos = lax.axis_index("head")
    ctx_pos = lax.axis_index("ctx")
    count = lax.axis_size("ctx")
    flag = jnp.stack([head_pos >> 1 & 1, ctx_pos]).astype(jnp.int32)

    proj_t = state_proj.T
    far_raw = swapped(proj_t, "head", 2)
    near_raw = swapped(proj_t, "head", 1)
    halo = rotated(tails(x_stream, proj_t, conv_proj), "ctx", 1)
    run, whole, step, totals, skip = decays(dt_raw.T, dt_bias, a_log, skip_d, chans)
    halves = 2
    x_two, v_two, mark = chan_conv(flag, x_stream, conv_x, run, step, None, 1, halves)
    halo = after(halo, mark)
    halo_far = swapped(halo, "head", 2)
    halo_near = swapped(halo, "head", 1)
    far_raw = after(far_raw, mark)
    cross_raw = swapped(far_raw, "head", 1)
    halo_cross = swapped(halo_far, "head", 1)
    x_one, v_one, mark = chan_conv(flag, x_stream, conv_x, run, step, halo, 0, halves)
    own = proj_conv(flag, proj_t, halo)
    near = proj_conv(flag, near_raw, halo_near)
    far = proj_conv(flag, after(far_raw, mark, own, near), halo_far)
    cross = proj_conv(flag, after(cross_raw, far), halo_cross)
    quarters = (own, near, far, cross)

    entering, message = states(flag, (v_one, v_two), quarters, totals)

    up = down = message
    ahead, behind, locs = [], [], []
    parts = count // 2
    per = parts // halves
    for at in range(parts):
        up = rotated(up, "ctx", 1)
        ahead.append(up)
        if at + 1 < count - parts:
            down = rotated(down, "ctx", -1)
            behind.append(down)
        piece = local(
            flag, (x_one, x_two)[at // per], quarters, entering, run, step, skip, at, parts,
            at % per * (tokens // parts // BLK),
        )
        if at + 1 < parts:
            up, down, piece = lax.optimization_barrier((up, down, piece))
        locs.append(piece)
    msgs = ahead + behind[::-1]

    width = HEADS // GROUPS * (chans // heads)
    gated, squares = carry(flag, locs, gate_z, quarters, whole, msgs)
    squares = (squares + swapped(squares, "head", 1)) + (
        swapped(squares, "head", 2) + swapped(squares, "head", 3)
    )
    return norm(gated, squares, norm_gain[None, :], width)


def solution(mesh):
    return jax.shard_map(
        on_device,
        mesh=mesh,
        in_specs=(
            P("ctx", "head"),
            P("ctx", "head"),
            P("ctx", "head"),
            P("ctx", "head"),
            P("head"),
            P("head"),
            P("head"),
            P(None, "head"),
            P(None, "head"),
            P("head"),
        ),
        out_specs=P("ctx", "head"),
        check_vma=False,
    )
```

```python
import jax
import jax.numpy as jnp
from jax import lax
from jax.experimental import pallas as pl
from jax.experimental.pallas import tpu as pltpu
from jax.sharding import PartitionSpec as P

HEADS = 256
STATE = 128
GROUPS = 8
BLK = 128
LOG2E = 1.4426950408889634
F32 = jnp.float32
BF16 = jnp.bfloat16
HIGH = lax.Precision.HIGHEST
VMEM_CAP = 8 * 1024 * 1024
LOCAL_UNROLL = 8
CARRY_UNROLL = 8
CONV_UNROLL = (7, 8)
STATE_UNROLL = 8


def shifted(x, axis, by):
    count = lax.axis_size(axis)
    pairs = [(i, i + by) for i in range(count) if 0 <= i + by < count]
    return lax.ppermute(x, axis, pairs)


def rotated(x, axis, by):
    count = lax.axis_size(axis)
    return lax.ppermute(x, axis, [(i, (i + by) % count) for i in range(count)])


def opposed(x, by):
    ctx, head = lax.axis_size("ctx"), lax.axis_size("head")
    pairs = []
    for i in range(ctx):
        for j in range(head):
            to = (i + (by if j % 2 == 0 else -by)) % ctx
            pairs.append((i * head + j, to * head + j))
    return lax.ppermute(x, ("ctx", "head"), pairs)


def swapped(value, axis, mask):
    return lax.ppermute(value, axis, [(i, i ^ mask) for i in range(lax.axis_size(axis))])


def after(value, *others):
    return lax.optimization_barrier((value,) + others)[0]


def params():
    return pltpu.CompilerParams(vmem_limit_bytes=VMEM_CAP)


def cost(flops, size, trans=0):
    return pl.CostEstimate(flops=flops, bytes_accessed=size, transcendentals=trans)


def specs(count, scalars=0):
    smem = pl.BlockSpec(memory_space=pltpu.SMEM)
    return [smem] * scalars + [pl.BlockSpec(memory_space=pltpu.VMEM)] * (count - scalars)


def half_silu(h):
    return h + h * jnp.tanh(h)


def iota(shape, dim):
    return lax.broadcasted_iota(jnp.int32, shape, dim)


def block_at(i):
    return pl.ds(pl.multiple_of(i * BLK, BLK), BLK)


def head_spread(heads, chans):
    return (iota((heads, chans), 1) // (chans // heads) == iota((heads, chans), 0)).astype(BF16)


def upright(row):
    count = row.shape[1]
    eye = iota((count, count), 0) == iota((count, count), 1)
    return jnp.sum(jnp.where(eye, row, 0.0), axis=1, keepdims=True)


def tails_kernel(x_ref, p_ref, w_ref, o_ref):
    half, chans = p_ref.shape[0], x_ref.shape[1]
    o_ref[0:half, :] = p_ref[...]
    for at in range(chans // BLK):
        lo = half + 16 * at
        o_ref[lo : lo + 16, :] = x_ref[:, at * BLK : (at + 1) * BLK]
    at = half + 16 * (chans // BLK)
    o_ref[at : at + 16, :] = jnp.zeros((16, BLK), BF16)
    o_ref[at : at + 4, 0:half] = w_ref[...]


def tails(x, proj_t, taps):
    tokens, chans = x.shape
    half = proj_t.shape[0]
    rows = half + 16 * (chans // BLK) + 16
    return pl.pallas_call(
        tails_kernel,
        grid=(1,),
        in_specs=[
            pl.BlockSpec((16, chans), lambda i: (tokens // 16 - 1, 0)),
            pl.BlockSpec((half, BLK), lambda i: (0, tokens // BLK - 1)),
            pl.BlockSpec(taps.shape, lambda i: (0, 0)),
        ],
        out_specs=pl.BlockSpec((rows, BLK), lambda i: (0, 0)),
        out_shape=jax.ShapeDtypeStruct((rows, BLK), BF16),
        compiler_params=pltpu.CompilerParams(vmem_limit_bytes=60 * 1024 * 1024),
        name="tails",
    )(x, proj_t, taps)


def proj_conv_kernel(
    wanted, flag_ref, own_ref, near_ref, far_ref, cross_ref, h0_ref, h1_ref, h2_ref, h3_ref, o_ref,
    tap_ref
):
    half, tokens = own_ref.shape
    here = flag_ref[0] == wanted

    def raw(at):
        return jnp.where(
            here,
            jnp.concatenate([own_ref[:, at], near_ref[:, at]], axis=0),
            jnp.concatenate([far_ref[:, at], cross_ref[:, at]], axis=0),
        )

    def of_halo(rows):
        return (
            jnp.where(here, h0_ref[rows, :], h2_ref[rows, :]),
            jnp.where(here, h1_ref[rows, :], h3_ref[rows, :]),
        )

    at = h0_ref.shape[0] - 16
    for q, weights in enumerate(of_halo(slice(at, at + 16))):
        columns = jnp.transpose(0.5 * weights.astype(F32)[0:8])
        for k in range(4):
            tap_ref[k, q * half : (q + 1) * half, :] = jnp.broadcast_to(
                columns[0:half, k : k + 1], (half, BLK)
            )
    before = jnp.concatenate(of_halo(slice(0, half)), axis=0)
    before = jnp.where(flag_ref[1] == 0, jnp.zeros_like(before), before)
    src, dst = iota((2 * BLK, 4 * BLK), 0), iota((2 * BLK, 4 * BLK), 1)
    shift = (src == BLK + dst % BLK - dst // BLK).astype(BF16)
    for i in range(tokens // BLK):
        cur = slice(i * BLK, (i + 1) * BLK)
        if i == 0:
            window = jnp.concatenate([before, raw(cur)], axis=1)
        else:
            window = raw(slice((i - 1) * BLK, (i + 1) * BLK))
        moved = jnp.dot(window, shift, preferred_element_type=F32)
        h = tap_ref[3] * moved[:, 0:BLK]
        for k in (1, 2, 3):
            h = h + tap_ref[3 - k] * moved[:, k * BLK : (k + 1) * BLK]
        o_ref[:, cur] = half_silu(h).astype(BF16)


def proj_conv(flag, raws, halos, wanted):
    half, tokens = raws[0].shape

    def kernel(*refs):
        proj_conv_kernel(wanted, *refs)

    return pl.pallas_call(
        kernel,
        in_specs=specs(9, 1),
        out_specs=specs(1)[0],
        out_shape=jax.ShapeDtypeStruct((2 * half, tokens), BF16),
        scratch_shapes=[pltpu.VMEM((4, 2 * half, BLK), F32)],
        compiler_params=params(),
        cost_estimate=cost(half * tokens * 4000, half * tokens * 6, half * tokens * 2),
        name="proj_conv",
    )(flag, *raws, *halos)


def decay_kernel(
    dt_ref, bias_ref, alog_ref, skip_ref, run_ref, abs_ref, step_ref, tot_ref, wide_ref
):
    heads, tokens = dt_ref.shape
    blocks = tokens // BLK
    chans = tot_ref.shape[1]
    raw = dt_ref[...] + upright(bias_ref[...])
    step = jnp.maximum(raw, 0.0) + jnp.log1p(jnp.exp(-jnp.abs(raw)))
    step_ref[...] = step
    log_decay = step * (-LOG2E * jnp.exp(upright(alog_ref[...])))
    stack = jnp.concatenate(
        [log_decay[:, b * BLK : (b + 1) * BLK] for b in range(blocks)], axis=0
    )
    upper = (iota((BLK, BLK), 0) <= iota((BLK, BLK), 1)).astype(F32)
    run = jnp.dot(stack, upper, precision=HIGH, preferred_element_type=F32)
    total = run[:, BLK - 1 : BLK]
    count = blocks * heads
    r, c = iota((count, count), 0), iota((count, count), 1)
    before = ((c // heads < r // heads) & (c % heads == r % heads)).astype(F32)
    start = jnp.dot(
        before,
        jnp.broadcast_to(total, (count, BLK)),
        precision=HIGH,
        preferred_element_type=F32,
    )
    whole = run + start
    for b in range(blocks):
        run_ref[:, b * BLK : (b + 1) * BLK] = run[b * heads : (b + 1) * heads]
        abs_ref[:, b * BLK : (b + 1) * BLK] = whole[b * heads : (b + 1) * heads]
    pick = (iota((blocks, count), 1) // heads == iota((blocks, count), 0)).astype(F32)
    chan_head = iota((count, chans), 1) // (chans // heads)
    spread = jnp.where(chan_head == iota((count, chans), 0) % heads, total, 0.0)
    own = iota((heads, chans), 1) // (chans // heads) == iota((heads, chans), 0)
    wide_ref[...] = jnp.sum(
        jnp.where(own, upright(skip_ref[...]), 0.0), axis=0, keepdims=True
    )
    tot_ref[...] = jnp.dot(pick, spread, precision=HIGH, preferred_element_type=F32)


def decays(dt_t, bias, a_log, skip, chans):
    heads, tokens = dt_t.shape
    rows = jax.ShapeDtypeStruct((heads, tokens), F32)
    return pl.pallas_call(
        decay_kernel,
        in_specs=specs(4),
        out_specs=tuple(specs(5)),
        out_shape=(
            rows,
            rows,
            rows,
            jax.ShapeDtypeStruct((tokens // BLK, chans), F32),
            jax.ShapeDtypeStruct((1, chans), F32),
        ),
        compiler_params=params(),
        cost_estimate=cost(heads * tokens * 20000, heads * tokens * 16, heads * tokens * 2),
        name="decays",
    )(dt_t, bias[None, :], a_log[None, :], skip[None, :])


def chan_conv_kernel(base, flag_ref, x_ref, w_ref, run_ref, step_ref, *rest):
    o_ref, v_ref, t_ref = rest[-3:]
    halo_ref = rest[0]
    chans = x_ref.shape[1]
    heads = run_ref.shape[0]
    count = o_ref.shape[0] // BLK
    spread = head_spread(heads, chans)

    def block(i, tails):
        src, dst = block_at(base + i), block_at(i)
        run = run_ref[:, src]
        coef = (jnp.exp2(run[:, BLK - 1 : BLK] - run) * step_ref[:, src]).astype(BF16)
        wide = lax.dot_general(
            coef, spread, (((0,), (0,)), ((), ())), preferred_element_type=F32
        )
        for at in range(chans // BLK):
            lanes = slice(at * BLK, (at + 1) * BLK)
            taps = [0.5 * w_ref[k : k + 1, lanes].astype(F32) for k in range(4)]
            cur = x_ref[src, lanes].astype(F32)
            ext = jnp.concatenate([tails(at).astype(F32)[8:16], cur], axis=0)
            back = pltpu.roll(ext, 1, 0)
            older = pltpu.roll(taps[1] * ext + taps[0] * back, 2, 0)
            y = half_silu(taps[3] * cur + taps[2] * back[8:] + older[8:])
            o_ref[dst, lanes] = y.astype(BF16)
            v_ref[dst, lanes] = (y * wide[:, lanes]).astype(BF16)

    def from_halo(at):
        lo = halo_ref.shape[0] - 16 - 16 * (chans // BLK) + 16 * at
        part = halo_ref[lo : lo + 16, :]
        return jnp.where(flag_ref[1] == 0, jnp.zeros_like(part), part)

    def inner(i):
        def tail(at):
            lo = pl.multiple_of((base + i) * BLK - 16, 16)
            return x_ref[pl.ds(lo, 16), at * BLK : (at + 1) * BLK]

        block(i, tail)

    first = 1 if base == 0 else 0
    if first:
        block(0, from_halo)

    @pl.loop(first, count, unroll=CONV_UNROLL[0] if first else CONV_UNROLL[1])
    def _(i):
        inner(i)

    t_ref[...] = jnp.zeros_like(t_ref)


def chan_conv(flag, x, taps, run, step, halo, part, parts):
    tokens, chans = x.shape
    here = tokens // parts

    def kernel(*refs):
        chan_conv_kernel(part * here // BLK, *refs)

    return pl.pallas_call(
        kernel,
        in_specs=specs(5 + (part == 0), 1),
        out_specs=tuple(specs(3)),
        out_shape=(jax.ShapeDtypeStruct((here, chans), BF16),) * 2
        + (jax.ShapeDtypeStruct((8, BLK), F32),),
        compiler_params=params(),
        cost_estimate=cost(here * chans * 4000, here * chans * 6, here * chans),
        name="chan_conv",
    )(flag, x, taps, run, step, *([halo] if part == 0 else []))


def write_log(msg_ref, log):
    high = log.astype(BF16).astype(F32)
    mid = (log - high).astype(BF16).astype(F32)
    low = (log - high) - mid
    row = iota((16, log.shape[1]), 0)
    parts = jnp.where(row == 0, high, jnp.where(row == 1, mid, jnp.where(row == 2, low, 0.0)))
    msg_ref[STATE : STATE + 16, :] = parts.astype(BF16)


def read_log(msg_ref):
    parts = msg_ref[STATE : STATE + 16, :].astype(F32)
    return (parts[0:1] + parts[1:2]) + parts[2:3]


def merge_kernel(level, devices, flag_ref, mine_ref, got_ref, o_ref):
    pos = flag_ref[1]
    even = flag_ref[2] == 0
    reach = 1 if level == 1 else 3
    keep_even = pos >= level
    keep_odd = pos + reach < devices
    if level == 2:
        keep_odd = keep_odd | (pos == devices - 1)
    keep = jnp.where(jnp.where(even, keep_even, keep_odd), 1.0, 0.0)
    mine_log, got_log = read_log(mine_ref), read_log(got_ref)
    early_log = keep * jnp.where(even, got_log, mine_log)
    late_log = jnp.where(even, mine_log, got_log)
    factor = keep * jnp.exp2(late_log)
    mine, got = mine_ref[0:STATE, :].astype(F32), got_ref[0:STATE, :].astype(F32)
    state = jnp.where(even, mine, got) + factor * jnp.where(even, got, mine)
    o_ref[0:STATE, :] = state.astype(BF16)
    write_log(o_ref, late_log + early_log)


def merge(flag, mine, got, level, devices):
    def kernel(*refs):
        merge_kernel(level, devices, *refs)

    return pl.pallas_call(
        kernel,
        in_specs=specs(3, 1),
        out_specs=specs(1)[0],
        out_shape=jax.ShapeDtypeStruct(mine.shape, BF16),
        compiler_params=params(),
        cost_estimate=cost(mine.size * 4, mine.size * 6),
        name="merge",
    )(flag, mine, got)


def state_kernel(b_ref, tot_ref, *rest):
    s_ref, msg_ref, now_ref = rest[-3:]
    v_refs = rest[:-3]
    chans = s_ref.shape[2]
    now_ref[...] = jnp.zeros_like(now_ref)
    for at, v_ref in enumerate(v_refs):
        count = v_ref.shape[0] // BLK
        base = at * count

        @pl.loop(0, count, unroll=STATE_UNROLL)
        def _(i):
            b = b_ref[:, block_at(base + i)]
            add = jnp.dot(b, v_ref[block_at(i), :], preferred_element_type=F32)
            now = now_ref[...]
            s_ref[base + i] = now.astype(BF16)
            now_ref[...] = jnp.exp2(tot_ref[pl.ds(base + i, 1), :]) * now + add

    msg_ref[0:STATE, :] = now_ref[...].astype(BF16)
    write_log(msg_ref, jnp.sum(tot_ref[...], axis=0, keepdims=True))


def states(weighted, b_t, totals):
    blocks, chans = totals.shape
    return pl.pallas_call(
        state_kernel,
        in_specs=specs(2 + len(weighted)),
        out_specs=tuple(specs(2)),
        out_shape=(
            jax.ShapeDtypeStruct((blocks, STATE, chans), BF16),
            jax.ShapeDtypeStruct((STATE + 16, chans), BF16),
        ),
        scratch_shapes=[pltpu.VMEM((STATE, chans), F32)],
        compiler_params=params(),
        cost_estimate=cost(blocks * BLK * chans * 2000, blocks * BLK * chans * 4),
        name="states",
    )(b_t, totals, *weighted)


def local_kernel(
    base, offset, x_ref, b_ref, c_ref, s_ref, run_ref, step_ref, skip_ref, o_ref
):
    tokens, chans = o_ref.shape
    heads = run_ref.shape[0]
    causal = iota((BLK, BLK), 0) >= iota((BLK, BLK), 1)
    left = iota((2 * BLK, BLK), 1) < chans // heads

    @pl.loop(0, tokens // BLK, unroll=LOCAL_UNROLL)
    def _(i):
        at = block_at(base + i)
        c = jnp.transpose(c_ref[:, at])
        gram = jnp.dot(c, b_ref[:, at], preferred_element_type=F32)
        gram = jnp.where(causal, gram, 0.0).astype(BF16)
        run = run_ref[:, at]
        run_t = jnp.transpose(run)
        step = step_ref[:, at].astype(BF16)
        for pair in range(heads // 2):
            lanes = slice(pair * BLK, (pair + 1) * BLK)
            mats = []
            for h in (2 * pair, 2 * pair + 1):
                column = jnp.broadcast_to(run_t[:, h : h + 1], (BLK, BLK))
                gap = (column - run[h : h + 1, :]).astype(BF16)
                mats.append(jnp.exp2(jnp.minimum(gap, 0.0)) * gram * step[h : h + 1, :])
                mats.append(jnp.exp2(column.astype(BF16)) * c)
            lhs = jnp.concatenate(mats, axis=1)
            xs = x_ref[block_at(offset + i), lanes]
            both = jnp.concatenate([xs, s_ref[base + i, :, lanes]], axis=0)
            zero = jnp.zeros_like(both)
            rhs = jnp.concatenate(
                [jnp.where(left, both, zero), jnp.where(left, zero, both)], axis=0
            )
            out = jnp.dot(lhs, rhs, preferred_element_type=F32)
            out = out + skip_ref[:, lanes] * xs.astype(F32)
            o_ref[block_at(i), lanes] = out.astype(BF16)


def local(x_conv, b_t, c_t, entering, run, step, skip, part, parts, offset):
    heads, tokens = run.shape
    chans = x_conv.shape[1]
    here = tokens // parts

    def kernel(*refs):
        local_kernel(part * here // BLK, offset, *refs)

    return pl.pallas_call(
        kernel,
        in_specs=specs(7),
        out_specs=specs(1)[0],
        out_shape=jax.ShapeDtypeStruct((here, chans), BF16),
        compiler_params=params(),
        cost_estimate=cost(8000 * here * chans, here * chans * 6, here * heads * BLK * 2),
        name="local",
    )(x_conv, b_t, c_t, entering, run, step, skip)


def carry_kernel(nloc, devices, flag_ref, c_ref, abs_ref, z_ref, *rest):
    l_refs, msgs = rest[:nloc], rest[nloc:-3]
    g_ref, q_ref, s_ref = rest[-3:]
    chans = g_ref.shape[1]
    heads = abs_ref.shape[0]
    pos = flag_ref[1]
    even = flag_ref[2] == 0
    near_ref, mid_ref, wide_ref = msgs
    one = jnp.where(even, pos >= 1, pos + 1 >= devices)
    two = jnp.where(even, pos >= 2, pos + 3 >= devices)
    four = jnp.where(even, pos >= 4, pos >= 1)
    first_ok = jnp.where(jnp.where(even, four, one), 1.0, 0.0)
    mid_ok = jnp.where(two, 1.0, 0.0)
    last_ok = jnp.where(jnp.where(even, one, four), 1.0, 0.0)
    near_log, far_log = read_log(near_ref), read_log(wide_ref)
    last_fall = jnp.exp2(last_ok * jnp.where(even, near_log, far_log))
    mid_fall = jnp.exp2(mid_ok * read_log(mid_ref)) * last_fall * first_ok
    last_fall = last_fall * mid_ok
    near, wide = near_ref[0:STATE, :].astype(F32), wide_ref[0:STATE, :].astype(F32)
    total = last_ok * jnp.where(even, near, wide) + mid_fall * jnp.where(even, wide, near)
    s_ref[...] = (total + last_fall * mid_ref[0:STATE, :].astype(F32)).astype(BF16)
    spread = head_spread(heads, chans)
    done = 0
    for l_ref in l_refs:
        count = l_ref.shape[0] // BLK
        first = done
        done += count

        @pl.loop(0, count, unroll=CARRY_UNROLL)
        def _(i):
            at = block_at(first + i)
            c = jnp.transpose(c_ref[:, at])
            wide = lax.dot_general(
                jnp.exp2(abs_ref[:, at]).astype(BF16),
                spread,
                (((0,), (0,)), ((), ())),
                preferred_element_type=F32,
            )
            carried = jnp.dot(c, s_ref[...], preferred_element_type=F32)
            folded = None
            for lo in range(0, chans, BLK):
                lanes = slice(lo, lo + BLK)
                gated = l_ref[block_at(i), lanes].astype(F32) + wide[:, lanes] * carried[:, lanes]
                gated = gated * half_silu(0.5 * z_ref[at, lanes].astype(F32))
                g_ref[at, lanes] = gated.astype(BF16)
                square = gated * gated
                folded = square if folded is None else folded + square
            q_ref[pl.ds(first + i, 1), :] = jnp.sum(jnp.transpose(folded), axis=0, keepdims=True)


def carry(flag, locs, gate, c_t, whole, msgs, devices):
    heads, tokens = whole.shape
    chans = locs[0].shape[1]

    def kernel(*refs):
        carry_kernel(len(locs), devices, *refs)

    return pl.pallas_call(
        kernel,
        in_specs=specs(4 + len(locs) + len(msgs), 1),
        out_specs=tuple(specs(2)),
        scratch_shapes=[pltpu.VMEM((STATE, chans), BF16)],
        out_shape=(
            jax.ShapeDtypeStruct((tokens, chans), BF16),
            jax.ShapeDtypeStruct((tokens // BLK, BLK), F32),
        ),
        compiler_params=params(),
        cost_estimate=cost(4000 * tokens * chans, tokens * chans * 6, tokens * chans),
        name="carry",
    )(flag, c_t, whole, gate, *locs, *msgs)


def norm_kernel(width, g_ref, q_ref, gain_ref, o_ref):
    tokens, chans = o_ref.shape
    per = tokens // BLK
    first = pl.program_id(0) * per
    for i in range(per):
        at = slice(i * BLK, (i + 1) * BLK)
        scale = lax.rsqrt(q_ref[pl.ds(first + i, 1), :] * (1.0 / width) + 1e-05)
        column = jnp.transpose(jnp.broadcast_to(scale, (BLK, BLK)))
        for lo in range(0, chans, BLK):
            lanes = slice(lo, lo + BLK)
            g = g_ref[block_at(first + i), lanes].astype(F32)
            o_ref[at, lanes] = (g * column * gain_ref[:, lanes]).astype(BF16)


def norm(gated, squares, gain, width, rows=2048):
    tokens, chans = gated.shape

    def kernel(*refs):
        norm_kernel(width, *refs)

    return pl.pallas_call(
        kernel,
        grid=(tokens // rows,),
        in_specs=specs(3),
        out_specs=pl.BlockSpec((rows, chans), lambda i: (i, 0)),
        out_shape=jax.ShapeDtypeStruct((tokens, chans), BF16),
        compiler_params=params(),
        cost_estimate=cost(tokens * chans * 3, tokens * chans * 4),
        name="norm",
    )(gated, squares, gain)


def on_device(
    x_stream, gate_z, state_proj, dt_raw, dt_bias, a_log, skip_d, conv_x, conv_proj, norm_gain
):
    tokens, chans = x_stream.shape
    heads = dt_raw.shape[1]
    head_pos = lax.axis_index("head")
    ctx_pos = lax.axis_index("ctx")
    count = lax.axis_size("ctx")
    flag = jnp.stack([head_pos >> 1 & 1, ctx_pos, head_pos & 1]).astype(jnp.int32)

    proj_t = state_proj.T
    far_raw = swapped(proj_t, "head", 2)
    near_raw = swapped(proj_t, "head", 1)
    ends = tails(x_stream, proj_t, conv_proj)
    halo = rotated(ends, "ctx", 1)
    run, whole, step, totals, skip = decays(after(dt_raw.T, ends), dt_bias, a_log, skip_d, chans)

    def conv(part, *needs):
        return chan_conv(after(flag, *needs), x_stream, conv_x, run, step, halo, part, 4)

    x3, v3, mark = conv(3)
    halo = after(halo, mark)
    halo_far = swapped(halo, "head", 2)
    halo_near = swapped(halo, "head", 1)
    x2, v2, mark = conv(2, halo, mark)
    far_raw, halo_far = lax.optimization_barrier((far_raw, halo_far, mark))[:2]
    cross_raw = swapped(far_raw, "head", 1)
    halo_cross = swapped(halo_far, "head", 1)
    x1, v1, mark = conv(1, far_raw, halo_far)
    x0, v0, mark = conv(0, mark)
    raws = (proj_t, near_raw, far_raw, after(cross_raw, mark))
    halos = (halo, halo_near, halo_far, halo_cross)
    b_t = proj_conv(flag, raws, halos, 0)
    entering, message = states((v0, v1, v2, v3), b_t, totals)
    c_t = proj_conv(after(flag, message), raws, halos, 1)

    locs = []

    def piece(at, *needs):
        x_conv = (x0, x1, x2, x3)[at]
        locs.append(
            local(x_conv, b_t, c_t, entering, after(run, *needs), step, skip, at, 4, 0)
        )
        return locs[-1]

    one = opposed(message, 1)
    pair = merge(flag, message, after(one, c_t), 1, count)
    two = opposed(pair, 2)
    piece(0, pair)
    last = piece(1, pair)
    quad = merge(flag, pair, after(two, last), 2, count)
    four = opposed(quad, 4)
    piece(2, quad)
    last = piece(3, quad)
    msgs = (one, two, after(four, last))

    width = HEADS // GROUPS * (chans // heads)
    gated, squares = carry(flag, locs, gate_z, c_t, whole, msgs, count)
    squares = (squares + swapped(squares, "head", 1)) + (
        swapped(squares, "head", 2) + swapped(squares, "head", 3)
    )
    return norm(gated, squares, norm_gain[None, :], width)


def solution(mesh):
    return jax.shard_map(
        on_device,
        mesh=mesh,
        in_specs=(
            P("ctx", "head"),
            P("ctx", "head"),
            P("ctx", "head"),
            P("ctx", "head"),
            P("head"),
            P("head"),
            P("head"),
            P(None, "head"),
            P(None, "head"),
            P("head"),
        ),
        out_specs=P("ctx", "head"),
        check_vma=False,
    )
```

```python
import jax
import jax.numpy as jnp
from jax import lax
from jax.experimental import pallas as pl
from jax.experimental.pallas import tpu as pltpu
from jax.sharding import PartitionSpec as P

HEADS = 256
STATE = 128
GROUPS = 8
BLK = 128
LOG2E = 1.4426950408889634
F32 = jnp.float32
BF16 = jnp.bfloat16
HIGH = lax.Precision.HIGHEST
VMEM_CAP = 8 * 1024 * 1024
LOCAL_UNROLL = 8
CARRY_UNROLL = 8
CONV_UNROLL = (7, 8)
STATE_UNROLL = 8


def shifted(x, axis, by):
    count = lax.axis_size(axis)
    pairs = [(i, i + by) for i in range(count) if 0 <= i + by < count]
    return lax.ppermute(x, axis, pairs)


def rotated(x, axis, by):
    count = lax.axis_size(axis)
    return lax.ppermute(x, axis, [(i, (i + by) % count) for i in range(count)])


def opposed(x, by):
    ctx, head = lax.axis_size("ctx"), lax.axis_size("head")
    pairs = []
    for i in range(ctx):
        for j in range(head):
            to = (i + (by if j % 2 == 0 else -by)) % ctx
            pairs.append((i * head + j, to * head + j))
    return lax.ppermute(x, ("ctx", "head"), pairs)


def swapped(value, axis, mask):
    return lax.ppermute(value, axis, [(i, i ^ mask) for i in range(lax.axis_size(axis))])


def params():
    return pltpu.CompilerParams(vmem_limit_bytes=VMEM_CAP)


def cost(flops, size, trans=0):
    return pl.CostEstimate(flops=flops, bytes_accessed=size, transcendentals=trans)


def specs(count, scalars=0):
    smem = pl.BlockSpec(memory_space=pltpu.SMEM)
    return [smem] * scalars + [pl.BlockSpec(memory_space=pltpu.VMEM)] * (count - scalars)


def ordered(kernel, skip, extra):
    def call(*refs):
        return kernel(*refs[:skip], *refs[skip + extra :])

    return call


def unread(needs):
    return [pl.BlockSpec(memory_space=pl.ANY)] * len(needs)


def half_silu(h):
    return h + h * jnp.tanh(h)


def iota(shape, dim):
    return lax.broadcasted_iota(jnp.int32, shape, dim)


def block_at(i):
    return pl.ds(pl.multiple_of(i * BLK, BLK), BLK)


def head_spread(heads, chans):
    return (iota((heads, chans), 1) // (chans // heads) == iota((heads, chans), 0)).astype(BF16)


def upright(row):
    count = row.shape[1]
    eye = iota((count, count), 0) == iota((count, count), 1)
    return jnp.sum(jnp.where(eye, row, 0.0), axis=1, keepdims=True)


def tails_kernel(x_ref, p_ref, w_ref, o_ref):
    half, chans = p_ref.shape[0], x_ref.shape[1]
    o_ref[0:half, :] = p_ref[...]
    for at in range(chans // BLK):
        lo = half + 16 * at
        o_ref[lo : lo + 16, :] = x_ref[:, at * BLK : (at + 1) * BLK]
    at = half + 16 * (chans // BLK)
    o_ref[at : at + 16, :] = jnp.zeros((16, BLK), BF16)
    o_ref[at : at + 4, 0:half] = w_ref[...]


def tails(x, proj_t, taps):
    tokens, chans = x.shape
    half = proj_t.shape[0]
    rows = half + 16 * (chans // BLK) + 16
    return pl.pallas_call(
        tails_kernel,
        grid=(1,),
        in_specs=[
            pl.BlockSpec((16, chans), lambda i: (tokens // 16 - 1, 0)),
            pl.BlockSpec((half, BLK), lambda i: (0, tokens // BLK - 1)),
            pl.BlockSpec(taps.shape, lambda i: (0, 0)),
        ],
        out_specs=pl.BlockSpec((rows, BLK), lambda i: (0, 0)),
        out_shape=jax.ShapeDtypeStruct((rows, BLK), BF16),
        compiler_params=pltpu.CompilerParams(vmem_limit_bytes=60 * 1024 * 1024),
        cost_estimate=cost(2 << 30, 1 << 20),
        name="tails",
    )(x, proj_t, taps)


def proj_conv_kernel(
    wanted, flag_ref, own_ref, near_ref, far_ref, cross_ref, h0_ref, h1_ref, h2_ref, h3_ref, o_ref,
    tap_ref
):
    half, tokens = own_ref.shape
    here = flag_ref[0] == wanted

    def raw(at):
        return jnp.where(
            here,
            jnp.concatenate([own_ref[:, at], near_ref[:, at]], axis=0),
            jnp.concatenate([far_ref[:, at], cross_ref[:, at]], axis=0),
        )

    def of_halo(rows):
        return (
            jnp.where(here, h0_ref[rows, :], h2_ref[rows, :]),
            jnp.where(here, h1_ref[rows, :], h3_ref[rows, :]),
        )

    at = h0_ref.shape[0] - 16
    for q, weights in enumerate(of_halo(slice(at, at + 16))):
        columns = jnp.transpose(0.5 * weights.astype(F32)[0:8])
        for k in range(4):
            tap_ref[k, q * half : (q + 1) * half, :] = jnp.broadcast_to(
                columns[0:half, k : k + 1], (half, BLK)
            )
    before = jnp.concatenate(of_halo(slice(0, half)), axis=0)
    before = jnp.where(flag_ref[1] == 0, jnp.zeros_like(before), before)
    src, dst = iota((2 * BLK, 4 * BLK), 0), iota((2 * BLK, 4 * BLK), 1)
    shift = (src == BLK + dst % BLK - dst // BLK).astype(BF16)
    for i in range(tokens // BLK):
        cur = slice(i * BLK, (i + 1) * BLK)
        if i == 0:
            window = jnp.concatenate([before, raw(cur)], axis=1)
        else:
            window = raw(slice((i - 1) * BLK, (i + 1) * BLK))
        moved = jnp.dot(window, shift, preferred_element_type=F32)
        h = tap_ref[3] * moved[:, 0:BLK]
        for k in (1, 2, 3):
            h = h + tap_ref[3 - k] * moved[:, k * BLK : (k + 1) * BLK]
        o_ref[:, cur] = half_silu(h).astype(BF16)


def proj_conv(flag, raws, halos, wanted, needs=()):
    half, tokens = raws[0].shape

    def kernel(*refs):
        proj_conv_kernel(wanted, *refs)

    return pl.pallas_call(
        ordered(kernel, 9, len(needs)),
        in_specs=specs(9, 1) + unread(needs),
        out_specs=specs(1)[0],
        out_shape=jax.ShapeDtypeStruct((2 * half, tokens), BF16),
        scratch_shapes=[pltpu.VMEM((4, 2 * half, BLK), F32)],
        compiler_params=params(),
        cost_estimate=cost(half * tokens * 4000, half * tokens * 6, half * tokens * 2),
        name="proj_conv",
    )(flag, *raws, *halos, *needs)


def decay_kernel(
    dt_ref, bias_ref, alog_ref, skip_ref, run_ref, abs_ref, step_ref, tot_ref, wide_ref
):
    heads, tokens = dt_ref.shape
    blocks = tokens // BLK
    chans = tot_ref.shape[1]
    raw = dt_ref[...] + upright(bias_ref[...])
    step = jnp.maximum(raw, 0.0) + jnp.log1p(jnp.exp(-jnp.abs(raw)))
    step_ref[...] = step
    log_decay = step * (-LOG2E * jnp.exp(upright(alog_ref[...])))
    stack = jnp.concatenate(
        [log_decay[:, b * BLK : (b + 1) * BLK] for b in range(blocks)], axis=0
    )
    upper = (iota((BLK, BLK), 0) <= iota((BLK, BLK), 1)).astype(F32)
    run = jnp.dot(stack, upper, precision=HIGH, preferred_element_type=F32)
    total = run[:, BLK - 1 : BLK]
    count = blocks * heads
    r, c = iota((count, count), 0), iota((count, count), 1)
    before = ((c // heads < r // heads) & (c % heads == r % heads)).astype(F32)
    start = jnp.dot(
        before,
        jnp.broadcast_to(total, (count, BLK)),
        precision=HIGH,
        preferred_element_type=F32,
    )
    whole = run + start
    for b in range(blocks):
        run_ref[:, b * BLK : (b + 1) * BLK] = run[b * heads : (b + 1) * heads]
        abs_ref[:, b * BLK : (b + 1) * BLK] = whole[b * heads : (b + 1) * heads]
    pick = (iota((blocks, count), 1) // heads == iota((blocks, count), 0)).astype(F32)
    chan_head = iota((count, chans), 1) // (chans // heads)
    spread = jnp.where(chan_head == iota((count, chans), 0) % heads, total, 0.0)
    own = iota((heads, chans), 1) // (chans // heads) == iota((heads, chans), 0)
    wide_ref[...] = jnp.sum(
        jnp.where(own, upright(skip_ref[...]), 0.0), axis=0, keepdims=True
    )
    tot_ref[...] = jnp.dot(pick, spread, precision=HIGH, preferred_element_type=F32)


def decays(dt_t, bias, a_log, skip, chans, needs=()):
    heads, tokens = dt_t.shape
    rows = jax.ShapeDtypeStruct((heads, tokens), F32)
    return pl.pallas_call(
        ordered(decay_kernel, 4, len(needs)),
        in_specs=specs(4) + unread(needs),
        out_specs=tuple(specs(5)),
        out_shape=(
            rows,
            rows,
            rows,
            jax.ShapeDtypeStruct((tokens // BLK, chans), F32),
            jax.ShapeDtypeStruct((1, chans), F32),
        ),
        compiler_params=params(),
        cost_estimate=cost(heads * tokens * 80000, heads * tokens * 16, heads * tokens * 2),
        name="decays",
    )(dt_t, bias[None, :], a_log[None, :], skip[None, :], *needs)


def chan_conv_kernel(base, flag_ref, x_ref, w_ref, run_ref, step_ref, *rest):
    o_ref, v_ref, t_ref = rest[-3:]
    halo_ref = rest[0]
    chans = x_ref.shape[1]
    heads = run_ref.shape[0]
    count = o_ref.shape[0] // BLK
    spread = head_spread(heads, chans)

    def block(i, tails):
        src, dst = block_at(base + i), block_at(i)
        run = run_ref[:, src]
        coef = (jnp.exp2(run[:, BLK - 1 : BLK] - run) * step_ref[:, src]).astype(BF16)
        wide = lax.dot_general(
            coef, spread, (((0,), (0,)), ((), ())), preferred_element_type=F32
        )
        for at in range(chans // BLK):
            lanes = slice(at * BLK, (at + 1) * BLK)
            taps = [0.5 * w_ref[k : k + 1, lanes].astype(F32) for k in range(4)]
            cur = x_ref[src, lanes].astype(F32)
            ext = jnp.concatenate([tails(at).astype(F32)[8:16], cur], axis=0)
            back = pltpu.roll(ext, 1, 0)
            older = pltpu.roll(taps[1] * ext + taps[0] * back, 2, 0)
            y = half_silu(taps[3] * cur + taps[2] * back[8:] + older[8:])
            o_ref[dst, lanes] = y.astype(BF16)
            v_ref[dst, lanes] = (y * wide[:, lanes]).astype(BF16)

    def from_halo(at):
        lo = halo_ref.shape[0] - 16 - 16 * (chans // BLK) + 16 * at
        part = halo_ref[lo : lo + 16, :]
        return jnp.where(flag_ref[1] == 0, jnp.zeros_like(part), part)

    def inner(i):
        def tail(at):
            lo = pl.multiple_of((base + i) * BLK - 16, 16)
            return x_ref[pl.ds(lo, 16), at * BLK : (at + 1) * BLK]

        block(i, tail)

    first = 1 if base == 0 else 0
    if first:
        block(0, from_halo)

    @pl.loop(first, count, unroll=CONV_UNROLL[0] if first else CONV_UNROLL[1])
    def _(i):
        inner(i)

    t_ref[...] = jnp.zeros_like(t_ref)


def chan_conv(flag, x, taps, run, step, halo, part, parts, needs=()):
    tokens, chans = x.shape
    here = tokens // parts

    def kernel(*refs):
        chan_conv_kernel(part * here // BLK, *refs)

    return pl.pallas_call(
        ordered(kernel, 5 + (part == 0), len(needs)),
        in_specs=specs(5 + (part == 0), 1) + unread(needs),
        out_specs=tuple(specs(3)),
        out_shape=(jax.ShapeDtypeStruct((here, chans), BF16),) * 2
        + (jax.ShapeDtypeStruct((8, BLK), F32),),
        compiler_params=params(),
        cost_estimate=cost(here * chans * 4000, here * chans * 6, here * chans),
        name="chan_conv",
    )(flag, x, taps, run, step, *([halo] if part == 0 else []), *needs)


def write_log(msg_ref, log):
    high = log.astype(BF16).astype(F32)
    mid = (log - high).astype(BF16).astype(F32)
    low = (log - high) - mid
    row = iota((16, log.shape[1]), 0)
    parts = jnp.where(row == 0, high, jnp.where(row == 1, mid, jnp.where(row == 2, low, 0.0)))
    msg_ref[STATE : STATE + 16, :] = parts.astype(BF16)


def read_log(msg_ref):
    parts = msg_ref[STATE : STATE + 16, :].astype(F32)
    return (parts[0:1] + parts[1:2]) + parts[2:3]


def merge_kernel(level, devices, flag_ref, mine_ref, got_ref, o_ref):
    pos = flag_ref[1]
    even = flag_ref[2] == 0
    reach = 1 if level == 1 else 3
    keep_even = pos >= level
    keep_odd = pos + reach < devices
    if level == 2:
        keep_odd = keep_odd | (pos == devices - 1)
    keep = jnp.where(jnp.where(even, keep_even, keep_odd), 1.0, 0.0)
    mine_log, got_log = read_log(mine_ref), read_log(got_ref)
    early_log = keep * jnp.where(even, got_log, mine_log)
    late_log = jnp.where(even, mine_log, got_log)
    factor = keep * jnp.exp2(late_log)
    mine, got = mine_ref[0:STATE, :].astype(F32), got_ref[0:STATE, :].astype(F32)
    state = jnp.where(even, mine, got) + factor * jnp.where(even, got, mine)
    o_ref[0:STATE, :] = state.astype(BF16)
    write_log(o_ref, late_log + early_log)


def merge(flag, mine, got, level, devices, needs=()):
    def kernel(*refs):
        merge_kernel(level, devices, *refs)

    return pl.pallas_call(
        ordered(kernel, 3, len(needs)),
        in_specs=specs(3, 1) + unread(needs),
        out_specs=specs(1)[0],
        out_shape=jax.ShapeDtypeStruct(mine.shape, BF16),
        compiler_params=params(),
        cost_estimate=cost(mine.size * 4, mine.size * 6),
        name="merge",
    )(flag, mine, got, *needs)


def state_kernel(b_ref, tot_ref, *rest):
    s_ref, msg_ref, now_ref = rest[-3:]
    v_refs = rest[:-3]
    chans = s_ref.shape[2]
    now_ref[...] = jnp.zeros_like(now_ref)
    for at, v_ref in enumerate(v_refs):
        count = v_ref.shape[0] // BLK
        base = at * count

        @pl.loop(0, count, unroll=STATE_UNROLL)
        def _(i):
            b = b_ref[:, block_at(base + i)]
            add = jnp.dot(b, v_ref[block_at(i), :], preferred_element_type=F32)
            now = now_ref[...]
            s_ref[base + i] = now.astype(BF16)
            now_ref[...] = jnp.exp2(tot_ref[pl.ds(base + i, 1), :]) * now + add

    msg_ref[0:STATE, :] = now_ref[...].astype(BF16)
    write_log(msg_ref, jnp.sum(tot_ref[...], axis=0, keepdims=True))


def states(weighted, b_t, totals):
    blocks, chans = totals.shape
    return pl.pallas_call(
        state_kernel,
        in_specs=specs(2 + len(weighted)),
        out_specs=tuple(specs(2)),
        out_shape=(
            jax.ShapeDtypeStruct((blocks, STATE, chans), BF16),
            jax.ShapeDtypeStruct((STATE + 16, chans), BF16),
        ),
        scratch_shapes=[pltpu.VMEM((STATE, chans), F32)],
        compiler_params=params(),
        cost_estimate=cost(blocks * BLK * chans * 2000, blocks * BLK * chans * 4),
        name="states",
    )(b_t, totals, *weighted)


def local_kernel(
    base, offset, x_ref, b_ref, c_ref, s_ref, run_ref, step_ref, skip_ref, o_ref
):
    tokens, chans = o_ref.shape
    heads = run_ref.shape[0]
    causal = iota((BLK, BLK), 0) >= iota((BLK, BLK), 1)
    left = iota((2 * BLK, BLK), 1) < chans // heads

    @pl.loop(0, tokens // BLK, unroll=LOCAL_UNROLL)
    def _(i):
        at = block_at(base + i)
        c = jnp.transpose(c_ref[:, at])
        gram = jnp.dot(c, b_ref[:, at], preferred_element_type=F32)
        gram = jnp.where(causal, gram, 0.0).astype(BF16)
        run = run_ref[:, at]
        run_t = jnp.transpose(run)
        step = step_ref[:, at].astype(BF16)
        for pair in range(heads // 2):
            lanes = slice(pair * BLK, (pair + 1) * BLK)
            mats = []
            for h in (2 * pair, 2 * pair + 1):
                column = jnp.broadcast_to(run_t[:, h : h + 1], (BLK, BLK))
                gap = (column - run[h : h + 1, :]).astype(BF16)
                mats.append(jnp.exp2(jnp.minimum(gap, 0.0)) * gram * step[h : h + 1, :])
                mats.append(jnp.exp2(column.astype(BF16)) * c)
            lhs = jnp.concatenate(mats, axis=1)
            xs = x_ref[block_at(offset + i), lanes]
            both = jnp.concatenate([xs, s_ref[base + i, :, lanes]], axis=0)
            zero = jnp.zeros_like(both)
            rhs = jnp.concatenate(
                [jnp.where(left, both, zero), jnp.where(left, zero, both)], axis=0
            )
            out = jnp.dot(lhs, rhs, preferred_element_type=F32)
            out = out + skip_ref[:, lanes] * xs.astype(F32)
            o_ref[block_at(i), lanes] = out.astype(BF16)


def local(x_conv, b_t, c_t, entering, run, step, skip, part, parts, offset, needs=()):
    heads, tokens = run.shape
    chans = x_conv.shape[1]
    here = tokens // parts

    def kernel(*refs):
        local_kernel(part * here // BLK, offset, *refs)

    return pl.pallas_call(
        ordered(kernel, 7, len(needs)),
        in_specs=specs(7) + unread(needs),
        out_specs=specs(1)[0],
        out_shape=jax.ShapeDtypeStruct((here, chans), BF16),
        compiler_params=params(),
        cost_estimate=cost(8000 * here * chans, here * chans * 6, here * heads * BLK * 2),
        name="local",
    )(x_conv, b_t, c_t, entering, run, step, skip, *needs)


def carry_kernel(nloc, devices, flag_ref, c_ref, abs_ref, z_ref, *rest):
    l_refs, msgs = rest[:nloc], rest[nloc:-3]
    g_ref, q_ref, s_ref = rest[-3:]
    chans = g_ref.shape[1]
    heads = abs_ref.shape[0]
    pos = flag_ref[1]
    even = flag_ref[2] == 0
    near_ref, mid_ref, wide_ref = msgs
    one = jnp.where(even, pos >= 1, pos + 1 >= devices)
    two = jnp.where(even, pos >= 2, pos + 3 >= devices)
    four = jnp.where(even, pos >= 4, pos >= 1)
    first_ok = jnp.where(jnp.where(even, four, one), 1.0, 0.0)
    mid_ok = jnp.where(two, 1.0, 0.0)
    last_ok = jnp.where(jnp.where(even, one, four), 1.0, 0.0)
    near_log, far_log = read_log(near_ref), read_log(wide_ref)
    last_fall = jnp.exp2(last_ok * jnp.where(even, near_log, far_log))
    mid_fall = jnp.exp2(mid_ok * read_log(mid_ref)) * last_fall * first_ok
    last_fall = last_fall * mid_ok
    near, wide = near_ref[0:STATE, :].astype(F32), wide_ref[0:STATE, :].astype(F32)
    total = last_ok * jnp.where(even, near, wide) + mid_fall * jnp.where(even, wide, near)
    s_ref[...] = (total + last_fall * mid_ref[0:STATE, :].astype(F32)).astype(BF16)
    spread = head_spread(heads, chans)
    done = 0
    for l_ref in l_refs:
        count = l_ref.shape[0] // BLK
        first = done
        done += count

        @pl.loop(0, count, unroll=CARRY_UNROLL)
        def _(i):
            at = block_at(first + i)
            c = jnp.transpose(c_ref[:, at])
            wide = lax.dot_general(
                jnp.exp2(abs_ref[:, at]).astype(BF16),
                spread,
                (((0,), (0,)), ((), ())),
                preferred_element_type=F32,
            )
            carried = jnp.dot(c, s_ref[...], preferred_element_type=F32)
            folded = None
            for lo in range(0, chans, BLK):
                lanes = slice(lo, lo + BLK)
                gated = l_ref[block_at(i), lanes].astype(F32) + wide[:, lanes] * carried[:, lanes]
                gated = gated * half_silu(0.5 * z_ref[at, lanes].astype(F32))
                g_ref[at, lanes] = gated.astype(BF16)
                square = gated * gated
                folded = square if folded is None else folded + square
            q_ref[pl.ds(first + i, 1), :] = jnp.sum(jnp.transpose(folded), axis=0, keepdims=True)


def carry(flag, locs, gate, c_t, whole, msgs, devices):
    heads, tokens = whole.shape
    chans = locs[0].shape[1]

    def kernel(*refs):
        carry_kernel(len(locs), devices, *refs)

    return pl.pallas_call(
        kernel,
        in_specs=specs(4 + len(locs) + len(msgs), 1),
        out_specs=tuple(specs(2)),
        scratch_shapes=[pltpu.VMEM((STATE, chans), BF16)],
        out_shape=(
            jax.ShapeDtypeStruct((tokens, chans), BF16),
            jax.ShapeDtypeStruct((tokens // BLK, BLK), F32),
        ),
        compiler_params=params(),
        cost_estimate=cost(4000 * tokens * chans, tokens * chans * 6, tokens * chans),
        name="carry",
    )(flag, c_t, whole, gate, *locs, *msgs)


def norm_kernel(width, g_ref, q_ref, gain_ref, o_ref):
    tokens, chans = o_ref.shape
    per = tokens // BLK
    first = pl.program_id(0) * per
    for i in range(per):
        at = slice(i * BLK, (i + 1) * BLK)
        scale = lax.rsqrt(q_ref[pl.ds(first + i, 1), :] * (1.0 / width) + 1e-05)
        column = jnp.transpose(jnp.broadcast_to(scale, (BLK, BLK)))
        for lo in range(0, chans, BLK):
            lanes = slice(lo, lo + BLK)
            g = g_ref[block_at(first + i), lanes].astype(F32)
            o_ref[at, lanes] = (g * column * gain_ref[:, lanes]).astype(BF16)


def norm(gated, squares, gain, width, rows=2048):
    tokens, chans = gated.shape

    def kernel(*refs):
        norm_kernel(width, *refs)

    return pl.pallas_call(
        kernel,
        grid=(tokens // rows,),
        in_specs=specs(3),
        out_specs=pl.BlockSpec((rows, chans), lambda i: (i, 0)),
        out_shape=jax.ShapeDtypeStruct((tokens, chans), BF16),
        compiler_params=params(),
        cost_estimate=cost(tokens * chans * 3, tokens * chans * 4),
        name="norm",
    )(gated, squares, gain)


def on_device(
    x_stream, gate_z, state_proj, dt_raw, dt_bias, a_log, skip_d, conv_x, conv_proj, norm_gain
):
    tokens, chans = x_stream.shape
    heads = dt_raw.shape[1]
    head_pos = lax.axis_index("head")
    ctx_pos = lax.axis_index("ctx")
    count = lax.axis_size("ctx")
    flag = jnp.stack([head_pos >> 1 & 1, ctx_pos, head_pos & 1]).astype(jnp.int32)

    proj_t = state_proj.T
    far_raw = swapped(proj_t, "head", 2)
    near_raw = swapped(proj_t, "head", 1)
    ends = tails(x_stream, proj_t, conv_proj)
    halo = rotated(ends, "ctx", 1)
    run, whole, step, totals, skip = decays(dt_raw.T, dt_bias, a_log, skip_d, chans, (ends,))

    def conv(part, *needs):
        return chan_conv(flag, x_stream, conv_x, run, step, halo, part, 4, needs)

    x3, v3, mark = conv(3)
    halo_far = swapped(halo, "head", 2)
    halo_near = swapped(halo, "head", 1)
    x2, v2, mark = conv(2, halo, mark)
    x1, v1, mark = conv(1, mark)
    far_raw, halo_far, mark = lax.optimization_barrier((far_raw, halo_far, mark))
    cross_raw = swapped(far_raw, "head", 1)
    halo_cross = swapped(halo_far, "head", 1)
    x0, v0, mark = conv(0, far_raw, halo_far, mark)
    cross_raw, mark = lax.optimization_barrier((cross_raw, mark))
    raws = (proj_t, near_raw, far_raw, cross_raw)
    halos = (halo, halo_near, halo_far, halo_cross)
    b_t = proj_conv(flag, raws, halos, 0)
    entering, message = states((v0, v1, v2, v3), b_t, totals)
    c_t = proj_conv(flag, raws, halos, 1, (message,))

    locs = []

    def piece(at, *needs):
        x_conv = (x0, x1, x2, x3)[at]
        locs.append(
            local(x_conv, b_t, c_t, entering, run, step, skip, at, 4, 0, needs)
        )
        return locs[-1]

    one = opposed(message, 1)
    pair = merge(flag, message, one, 1, count, (c_t,))
    two = opposed(pair, 2)
    piece(0, pair)
    last = piece(1, pair, locs[0])
    quad = merge(flag, pair, two, 2, count, (last,))
    four = opposed(quad, 4)
    piece(2, quad)
    piece(3, quad)
    msgs = (one, two, four)

    width = HEADS // GROUPS * (chans // heads)
    gated, squares = carry(flag, locs, gate_z, c_t, whole, msgs, count)
    squares = (squares + swapped(squares, "head", 1)) + (
        swapped(squares, "head", 2) + swapped(squares, "head", 3)
    )
    return norm(gated, squares, norm_gain[None, :], width)


def solution(mesh):
    return jax.shard_map(
        on_device,
        mesh=mesh,
        in_specs=(
            P("ctx", "head"),
            P("ctx", "head"),
            P("ctx", "head"),
            P("ctx", "head"),
            P("head"),
            P("head"),
            P("head"),
            P(None, "head"),
            P(None, "head"),
            P("head"),
        ),
        out_specs=P("ctx", "head"),
        check_vma=False,
    )
```

```python
import jax
import jax.numpy as jnp
from jax import lax
from jax.experimental import pallas as pl
from jax.experimental.pallas import tpu as pltpu
from jax.sharding import PartitionSpec as P

HEADS = 256
STATE = 128
GROUPS = 8
BLK = 128
LOG2E = 1.4426950408889634
F32 = jnp.float32
BF16 = jnp.bfloat16
HIGH = lax.Precision.HIGHEST
VMEM_CAP = 8 * 1024 * 1024
LOCAL_UNROLL = 8
CARRY_UNROLL = 8
CONV_UNROLL = (7, 8)
STATE_UNROLL = 8


def shifted(x, axis, by):
    count = lax.axis_size(axis)
    pairs = [(i, i + by) for i in range(count) if 0 <= i + by < count]
    return lax.ppermute(x, axis, pairs)


def rotated(x, axis, by):
    count = lax.axis_size(axis)
    return lax.ppermute(x, axis, [(i, (i + by) % count) for i in range(count)])


def opposed(x, by):
    ctx, head = lax.axis_size("ctx"), lax.axis_size("head")
    pairs = []
    for i in range(ctx):
        for j in range(head):
            to = (i + (by if j % 2 == 0 else -by)) % ctx
            pairs.append((i * head + j, to * head + j))
    return lax.ppermute(x, ("ctx", "head"), pairs)


def swapped(value, axis, mask):
    return lax.ppermute(value, axis, [(i, i ^ mask) for i in range(lax.axis_size(axis))])


def params():
    return pltpu.CompilerParams(vmem_limit_bytes=VMEM_CAP)


def cost(flops, size, trans=0):
    return pl.CostEstimate(flops=flops, bytes_accessed=size, transcendentals=trans)


def specs(count, scalars=0):
    smem = pl.BlockSpec(memory_space=pltpu.SMEM)
    return [smem] * scalars + [pl.BlockSpec(memory_space=pltpu.VMEM)] * (count - scalars)


def ordered(kernel, skip, extra):
    def call(*refs):
        return kernel(*refs[:skip], *refs[skip + extra :])

    return call


def unread(needs):
    return [pl.BlockSpec(memory_space=pl.ANY)] * len(needs)


def half_silu(h):
    return h + h * jnp.tanh(h)


def iota(shape, dim):
    return lax.broadcasted_iota(jnp.int32, shape, dim)


def block_at(i):
    return pl.ds(pl.multiple_of(i * BLK, BLK), BLK)


def head_spread(heads, chans):
    return (iota((heads, chans), 1) // (chans // heads) == iota((heads, chans), 0)).astype(BF16)


def upright(row):
    count = row.shape[1]
    eye = iota((count, count), 0) == iota((count, count), 1)
    return jnp.sum(jnp.where(eye, row, 0.0), axis=1, keepdims=True)


def tails_kernel(x_ref, p_ref, w_ref, o_ref):
    half, chans = p_ref.shape[0], x_ref.shape[1]
    o_ref[0:half, :] = p_ref[...]
    for at in range(chans // BLK):
        lo = half + 16 * at
        o_ref[lo : lo + 16, :] = x_ref[:, at * BLK : (at + 1) * BLK]
    at = half + 16 * (chans // BLK)
    o_ref[at : at + 16, :] = jnp.zeros((16, BLK), BF16)
    o_ref[at : at + 4, 0:half] = w_ref[...]


def tails(x, proj_t, taps):
    tokens, chans = x.shape
    half = proj_t.shape[0]
    rows = half + 16 * (chans // BLK) + 16
    return pl.pallas_call(
        tails_kernel,
        grid=(1,),
        in_specs=[
            pl.BlockSpec((16, chans), lambda i: (tokens // 16 - 1, 0)),
            pl.BlockSpec((half, BLK), lambda i: (0, tokens // BLK - 1)),
            pl.BlockSpec(taps.shape, lambda i: (0, 0)),
        ],
        out_specs=pl.BlockSpec((rows, BLK), lambda i: (0, 0)),
        out_shape=jax.ShapeDtypeStruct((rows, BLK), BF16),
        compiler_params=pltpu.CompilerParams(vmem_limit_bytes=60 * 1024 * 1024),
        cost_estimate=cost(2 << 30, 1 << 20),
        name="tails",
    )(x, proj_t, taps)


def proj_conv_kernel(
    wanted, flag_ref, own_ref, near_ref, far_ref, cross_ref, h0_ref, h1_ref, h2_ref, h3_ref, o_ref,
    tap_ref
):
    half, tokens = own_ref.shape
    here = flag_ref[0] == wanted

    def raw(at):
        return jnp.where(
            here,
            jnp.concatenate([own_ref[:, at], near_ref[:, at]], axis=0),
            jnp.concatenate([far_ref[:, at], cross_ref[:, at]], axis=0),
        )

    def of_halo(rows):
        return (
            jnp.where(here, h0_ref[rows, :], h2_ref[rows, :]),
            jnp.where(here, h1_ref[rows, :], h3_ref[rows, :]),
        )

    at = h0_ref.shape[0] - 16
    for q, weights in enumerate(of_halo(slice(at, at + 16))):
        columns = jnp.transpose(0.5 * weights.astype(F32)[0:8])
        for k in range(4):
            tap_ref[k, q * half : (q + 1) * half, :] = jnp.broadcast_to(
                columns[0:half, k : k + 1], (half, BLK)
            )
    before = jnp.concatenate(of_halo(slice(0, half)), axis=0)
    before = jnp.where(flag_ref[1] == 0, jnp.zeros_like(before), before)
    src, dst = iota((2 * BLK, 4 * BLK), 0), iota((2 * BLK, 4 * BLK), 1)
    shift = (src == BLK + dst % BLK - dst // BLK).astype(BF16)
    for i in range(tokens // BLK):
        cur = slice(i * BLK, (i + 1) * BLK)
        if i == 0:
            window = jnp.concatenate([before, raw(cur)], axis=1)
        else:
            window = raw(slice((i - 1) * BLK, (i + 1) * BLK))
        moved = jnp.dot(window, shift, preferred_element_type=F32)
        h = tap_ref[3] * moved[:, 0:BLK]
        for k in (1, 2, 3):
            h = h + tap_ref[3 - k] * moved[:, k * BLK : (k + 1) * BLK]
        o_ref[:, cur] = half_silu(h).astype(BF16)


def proj_conv(flag, raws, halos, wanted, needs=()):
    half, tokens = raws[0].shape

    def kernel(*refs):
        proj_conv_kernel(wanted, *refs)

    return pl.pallas_call(
        ordered(kernel, 9, len(needs)),
        in_specs=specs(9, 1) + unread(needs),
        out_specs=specs(1)[0],
        out_shape=jax.ShapeDtypeStruct((2 * half, tokens), BF16),
        scratch_shapes=[pltpu.VMEM((4, 2 * half, BLK), F32)],
        compiler_params=params(),
        cost_estimate=cost(half * tokens * 4000, half * tokens * 6, half * tokens * 2),
        name="proj_conv",
    )(flag, *raws, *halos, *needs)


def decay_kernel(
    dt_ref, bias_ref, alog_ref, skip_ref, run_ref, abs_ref, step_ref, tot_ref, wide_ref
):
    heads, tokens = dt_ref.shape
    blocks = tokens // BLK
    chans = tot_ref.shape[1]
    raw = dt_ref[...] + upright(bias_ref[...])
    step = jnp.maximum(raw, 0.0) + jnp.log1p(jnp.exp(-jnp.abs(raw)))
    step_ref[...] = step
    log_decay = step * (-LOG2E * jnp.exp(upright(alog_ref[...])))
    stack = jnp.concatenate(
        [log_decay[:, b * BLK : (b + 1) * BLK] for b in range(blocks)], axis=0
    )
    upper = (iota((BLK, BLK), 0) <= iota((BLK, BLK), 1)).astype(F32)
    run = jnp.dot(stack, upper, precision=HIGH, preferred_element_type=F32)
    total = run[:, BLK - 1 : BLK]
    count = blocks * heads
    r, c = iota((count, count), 0), iota((count, count), 1)
    before = ((c // heads < r // heads) & (c % heads == r % heads)).astype(F32)
    start = jnp.dot(
        before,
        jnp.broadcast_to(total, (count, BLK)),
        precision=HIGH,
        preferred_element_type=F32,
    )
    whole = run + start
    for b in range(blocks):
        run_ref[:, b * BLK : (b + 1) * BLK] = run[b * heads : (b + 1) * heads]
        abs_ref[:, b * BLK : (b + 1) * BLK] = whole[b * heads : (b + 1) * heads]
    pick = (iota((blocks, count), 1) // heads == iota((blocks, count), 0)).astype(F32)
    chan_head = iota((count, chans), 1) // (chans // heads)
    spread = jnp.where(chan_head == iota((count, chans), 0) % heads, total, 0.0)
    own = iota((heads, chans), 1) // (chans // heads) == iota((heads, chans), 0)
    wide_ref[...] = jnp.sum(
        jnp.where(own, upright(skip_ref[...]), 0.0), axis=0, keepdims=True
    )
    tot_ref[...] = jnp.dot(pick, spread, precision=HIGH, preferred_element_type=F32)


def decays(dt_t, bias, a_log, skip, chans, needs=()):
    heads, tokens = dt_t.shape
    rows = jax.ShapeDtypeStruct((heads, tokens), F32)
    return pl.pallas_call(
        ordered(decay_kernel, 4, len(needs)),
        in_specs=specs(4) + unread(needs),
        out_specs=tuple(specs(5)),
        out_shape=(
            rows,
            rows,
            rows,
            jax.ShapeDtypeStruct((tokens // BLK, chans), F32),
            jax.ShapeDtypeStruct((1, chans), F32),
        ),
        compiler_params=params(),
        cost_estimate=cost(heads * tokens * 80000, heads * tokens * 16, heads * tokens * 2),
        name="decays",
    )(dt_t, bias[None, :], a_log[None, :], skip[None, :], *needs)


def chan_conv_kernel(base, flag_ref, x_ref, w_ref, run_ref, step_ref, *rest):
    o_ref, v_ref, t_ref = rest[-3:]
    halo_ref = rest[0]
    chans = x_ref.shape[1]
    heads = run_ref.shape[0]
    count = o_ref.shape[0] // BLK
    spread = head_spread(heads, chans)

    def block(i, tails):
        src, dst = block_at(base + i), block_at(i)
        run = run_ref[:, src]
        coef = (jnp.exp2(run[:, BLK - 1 : BLK] - run) * step_ref[:, src]).astype(BF16)
        wide = lax.dot_general(
            coef, spread, (((0,), (0,)), ((), ())), preferred_element_type=F32
        )
        for at in range(chans // BLK):
            lanes = slice(at * BLK, (at + 1) * BLK)
            taps = [0.5 * w_ref[k : k + 1, lanes].astype(F32) for k in range(4)]
            cur = x_ref[src, lanes].astype(F32)
            ext = jnp.concatenate([tails(at).astype(F32)[8:16], cur], axis=0)
            back = pltpu.roll(ext, 1, 0)
            older = pltpu.roll(taps[1] * ext + taps[0] * back, 2, 0)
            y = half_silu(taps[3] * cur + taps[2] * back[8:] + older[8:])
            o_ref[dst, lanes] = y.astype(BF16)
            v_ref[dst, lanes] = (y * wide[:, lanes]).astype(BF16)

    def from_halo(at):
        lo = halo_ref.shape[0] - 16 - 16 * (chans // BLK) + 16 * at
        part = halo_ref[lo : lo + 16, :]
        return jnp.where(flag_ref[1] == 0, jnp.zeros_like(part), part)

    def inner(i):
        def tail(at):
            lo = pl.multiple_of((base + i) * BLK - 16, 16)
            return x_ref[pl.ds(lo, 16), at * BLK : (at + 1) * BLK]

        block(i, tail)

    first = 1 if base == 0 else 0
    if first:
        block(0, from_halo)

    @pl.loop(first, count, unroll=CONV_UNROLL[0] if first else CONV_UNROLL[1])
    def _(i):
        inner(i)

    t_ref[...] = jnp.zeros_like(t_ref)


def chan_conv(flag, x, taps, run, step, halo, part, parts, needs=()):
    tokens, chans = x.shape
    here = tokens // parts

    def kernel(*refs):
        chan_conv_kernel(part * here // BLK, *refs)

    return pl.pallas_call(
        ordered(kernel, 5 + (part == 0), len(needs)),
        in_specs=specs(5 + (part == 0), 1) + unread(needs),
        out_specs=tuple(specs(3)),
        out_shape=(jax.ShapeDtypeStruct((here, chans), BF16),) * 2
        + (jax.ShapeDtypeStruct((8, BLK), F32),),
        compiler_params=params(),
        cost_estimate=cost(here * chans * 4000, here * chans * 6, here * chans),
        name="chan_conv",
    )(flag, x, taps, run, step, *([halo] if part == 0 else []), *needs)


def write_log(msg_ref, log):
    high = log.astype(BF16).astype(F32)
    mid = (log - high).astype(BF16).astype(F32)
    low = (log - high) - mid
    row = iota((16, log.shape[1]), 0)
    parts = jnp.where(row == 0, high, jnp.where(row == 1, mid, jnp.where(row == 2, low, 0.0)))
    msg_ref[STATE : STATE + 16, :] = parts.astype(BF16)


def read_log(msg_ref):
    parts = msg_ref[STATE : STATE + 16, :].astype(F32)
    return (parts[0:1] + parts[1:2]) + parts[2:3]


def merge_kernel(level, devices, flag_ref, mine_ref, got_ref, o_ref):
    pos = flag_ref[1]
    even = flag_ref[2] == 0
    reach = 1 if level == 1 else 3
    keep_even = pos >= level
    keep_odd = pos + reach < devices
    if level == 2:
        keep_odd = keep_odd | (pos == devices - 1)
    keep = jnp.where(jnp.where(even, keep_even, keep_odd), 1.0, 0.0)
    mine_log, got_log = read_log(mine_ref), read_log(got_ref)
    early_log = keep * jnp.where(even, got_log, mine_log)
    late_log = jnp.where(even, mine_log, got_log)
    factor = keep * jnp.exp2(late_log)
    mine, got = mine_ref[0:STATE, :].astype(F32), got_ref[0:STATE, :].astype(F32)
    state = jnp.where(even, mine, got) + factor * jnp.where(even, got, mine)
    o_ref[0:STATE, :] = state.astype(BF16)
    write_log(o_ref, late_log + early_log)


def merge(flag, mine, got, level, devices, needs=()):
    def kernel(*refs):
        merge_kernel(level, devices, *refs)

    return pl.pallas_call(
        ordered(kernel, 3, len(needs)),
        in_specs=specs(3, 1) + unread(needs),
        out_specs=specs(1)[0],
        out_shape=jax.ShapeDtypeStruct(mine.shape, BF16),
        compiler_params=params(),
        cost_estimate=cost(mine.size * 4, mine.size * 6),
        name="merge",
    )(flag, mine, got, *needs)


def state_kernel(b_ref, tot_ref, *rest):
    s_ref, msg_ref, now_ref = rest[-3:]
    v_refs = rest[:-3]
    chans = s_ref.shape[2]
    now_ref[...] = jnp.zeros_like(now_ref)
    for at, v_ref in enumerate(v_refs):
        count = v_ref.shape[0] // BLK
        base = at * count

        @pl.loop(0, count, unroll=STATE_UNROLL)
        def _(i):
            b = b_ref[:, block_at(base + i)]
            add = jnp.dot(b, v_ref[block_at(i), :], preferred_element_type=F32)
            now = now_ref[...]
            s_ref[base + i] = now.astype(BF16)
            now_ref[...] = jnp.exp2(tot_ref[pl.ds(base + i, 1), :]) * now + add

    msg_ref[0:STATE, :] = now_ref[...].astype(BF16)
    write_log(msg_ref, jnp.sum(tot_ref[...], axis=0, keepdims=True))


def states(weighted, b_t, totals):
    blocks, chans = totals.shape
    return pl.pallas_call(
        state_kernel,
        in_specs=specs(2 + len(weighted)),
        out_specs=tuple(specs(2)),
        out_shape=(
            jax.ShapeDtypeStruct((blocks, STATE, chans), BF16),
            jax.ShapeDtypeStruct((STATE + 16, chans), BF16),
        ),
        scratch_shapes=[pltpu.VMEM((STATE, chans), F32)],
        compiler_params=params(),
        cost_estimate=cost(blocks * BLK * chans * 2000, blocks * BLK * chans * 4),
        name="states",
    )(b_t, totals, *weighted)


def local_kernel(
    base, offset, x_ref, b_ref, c_ref, s_ref, run_ref, step_ref, skip_ref, o_ref
):
    tokens, chans = o_ref.shape
    heads = run_ref.shape[0]
    causal = iota((BLK, BLK), 0) >= iota((BLK, BLK), 1)
    left = iota((2 * BLK, BLK), 1) < chans // heads

    @pl.loop(0, tokens // BLK, unroll=LOCAL_UNROLL)
    def _(i):
        at = block_at(base + i)
        c = jnp.transpose(c_ref[:, at])
        gram = jnp.dot(c, b_ref[:, at], preferred_element_type=F32)
        gram = jnp.where(causal, gram, 0.0).astype(BF16)
        run = run_ref[:, at]
        run_t = jnp.transpose(run)
        step = step_ref[:, at].astype(BF16)
        for pair in range(heads // 2):
            lanes = slice(pair * BLK, (pair + 1) * BLK)
            mats = []
            for h in (2 * pair, 2 * pair + 1):
                column = jnp.broadcast_to(run_t[:, h : h + 1], (BLK, BLK))
                gap = (column - run[h : h + 1, :]).astype(BF16)
                mats.append(jnp.exp2(jnp.minimum(gap, 0.0)) * gram * step[h : h + 1, :])
                mats.append(jnp.exp2(column.astype(BF16)) * c)
            lhs = jnp.concatenate(mats, axis=1)
            xs = x_ref[block_at(offset + i), lanes]
            both = jnp.concatenate([xs, s_ref[base + i, :, lanes]], axis=0)
            zero = jnp.zeros_like(both)
            rhs = jnp.concatenate(
                [jnp.where(left, both, zero), jnp.where(left, zero, both)], axis=0
            )
            out = jnp.dot(lhs, rhs, preferred_element_type=F32)
            out = out + skip_ref[:, lanes] * xs.astype(F32)
            o_ref[block_at(i), lanes] = out.astype(BF16)


def local(x_conv, b_t, c_t, entering, run, step, skip, part, parts, offset, needs=()):
    heads, tokens = run.shape
    chans = x_conv.shape[1]
    here = tokens // parts

    def kernel(*refs):
        local_kernel(part * here // BLK, offset, *refs)

    return pl.pallas_call(
        ordered(kernel, 7, len(needs)),
        in_specs=specs(7) + unread(needs),
        out_specs=specs(1)[0],
        out_shape=jax.ShapeDtypeStruct((here, chans), BF16),
        compiler_params=params(),
        cost_estimate=cost(8000 * here * chans, here * chans * 6, here * heads * BLK * 2),
        name="local",
    )(x_conv, b_t, c_t, entering, run, step, skip, *needs)


def gate_kernel(z_ref, abs_ref, g_ref, w_ref):
    tokens, chans = z_ref.shape
    spread = head_spread(abs_ref.shape[0], chans)

    @pl.loop(0, tokens // BLK, unroll=4)
    def _(i):
        at = block_at(i)
        wide = lax.dot_general(
            jnp.exp2(abs_ref[:, at]).astype(BF16),
            spread,
            (((0,), (0,)), ((), ())),
            preferred_element_type=F32,
        )
        for lo in range(0, chans, BLK):
            lanes = slice(lo, lo + BLK)
            gate = half_silu(0.5 * z_ref[at, lanes].astype(F32))
            g_ref[at, lanes] = gate.astype(BF16)
            w_ref[at, lanes] = (gate * wide[:, lanes]).astype(BF16)


def gates(z, whole, needs):
    tokens, chans = z.shape
    return pl.pallas_call(
        ordered(gate_kernel, 2, len(needs)),
        in_specs=specs(2) + unread(needs),
        out_specs=tuple(specs(2)),
        out_shape=(jax.ShapeDtypeStruct((tokens, chans), BF16),) * 2,
        compiler_params=params(),
        cost_estimate=cost(tokens * chans * 1500, tokens * chans * 6, tokens * chans),
        name="gates",
    )(z, whole, *needs)


def carry_kernel(nloc, devices, flag_ref, c_ref, gate_ref, fall_ref, *rest):
    l_refs, msgs = rest[:nloc], rest[nloc:-3]
    g_ref, q_ref, s_ref = rest[-3:]
    chans = g_ref.shape[1]
    pos = flag_ref[1]
    even = flag_ref[2] == 0
    near_ref, mid_ref, wide_ref = msgs
    one = jnp.where(even, pos >= 1, pos + 1 >= devices)
    two = jnp.where(even, pos >= 2, pos + 3 >= devices)
    four = jnp.where(even, pos >= 4, pos >= 1)
    first_ok = jnp.where(jnp.where(even, four, one), 1.0, 0.0)
    mid_ok = jnp.where(two, 1.0, 0.0)
    last_ok = jnp.where(jnp.where(even, one, four), 1.0, 0.0)
    near_log, far_log = read_log(near_ref), read_log(wide_ref)
    last_fall = jnp.exp2(last_ok * jnp.where(even, near_log, far_log))
    mid_fall = jnp.exp2(mid_ok * read_log(mid_ref)) * last_fall * first_ok
    last_fall = last_fall * mid_ok
    near, wide = near_ref[0:STATE, :].astype(F32), wide_ref[0:STATE, :].astype(F32)
    total = last_ok * jnp.where(even, near, wide) + mid_fall * jnp.where(even, wide, near)
    s_ref[...] = (total + last_fall * mid_ref[0:STATE, :].astype(F32)).astype(BF16)
    done = 0
    for l_ref in l_refs:
        count = l_ref.shape[0] // BLK
        first = done
        done += count

        @pl.loop(0, count, unroll=CARRY_UNROLL)
        def _(i):
            at = block_at(first + i)
            c = jnp.transpose(c_ref[:, at])
            carried = jnp.dot(c, s_ref[...], preferred_element_type=F32)
            folded = None
            for lo in range(0, chans, BLK):
                lanes = slice(lo, lo + BLK)
                gated = l_ref[block_at(i), lanes].astype(F32) * gate_ref[at, lanes].astype(F32)
                gated = gated + fall_ref[at, lanes].astype(F32) * carried[:, lanes]
                g_ref[at, lanes] = gated.astype(BF16)
                square = gated * gated
                folded = square if folded is None else folded + square
            q_ref[pl.ds(first + i, 1), :] = jnp.sum(jnp.transpose(folded), axis=0, keepdims=True)


def carry(flag, locs, gate, fall, c_t, msgs, devices):
    tokens, chans = gate.shape

    def kernel(*refs):
        carry_kernel(len(locs), devices, *refs)

    return pl.pallas_call(
        kernel,
        in_specs=specs(4 + len(locs) + len(msgs), 1),
        out_specs=tuple(specs(2)),
        scratch_shapes=[pltpu.VMEM((STATE, chans), BF16)],
        out_shape=(
            jax.ShapeDtypeStruct((tokens, chans), BF16),
            jax.ShapeDtypeStruct((tokens // BLK, BLK), F32),
        ),
        compiler_params=params(),
        cost_estimate=cost(4000 * tokens * chans, tokens * chans * 6, tokens * chans),
        name="carry",
    )(flag, c_t, gate, fall, *locs, *msgs)


def norm_kernel(width, g_ref, q_ref, gain_ref, o_ref):
    tokens, chans = o_ref.shape
    per = tokens // BLK
    first = pl.program_id(0) * per
    for i in range(per):
        at = slice(i * BLK, (i + 1) * BLK)
        scale = lax.rsqrt(q_ref[pl.ds(first + i, 1), :] * (1.0 / width) + 1e-05)
        column = jnp.transpose(jnp.broadcast_to(scale, (BLK, BLK)))
        for lo in range(0, chans, BLK):
            lanes = slice(lo, lo + BLK)
            g = g_ref[block_at(first + i), lanes].astype(F32)
            o_ref[at, lanes] = (g * column * gain_ref[:, lanes]).astype(BF16)


def norm(gated, squares, gain, width, rows=2048):
    tokens, chans = gated.shape

    def kernel(*refs):
        norm_kernel(width, *refs)

    return pl.pallas_call(
        kernel,
        grid=(tokens // rows,),
        in_specs=specs(3),
        out_specs=pl.BlockSpec((rows, chans), lambda i: (i, 0)),
        out_shape=jax.ShapeDtypeStruct((tokens, chans), BF16),
        compiler_params=params(),
        cost_estimate=cost(tokens * chans * 3, tokens * chans * 4),
        name="norm",
    )(gated, squares, gain)


def on_device(
    x_stream, gate_z, state_proj, dt_raw, dt_bias, a_log, skip_d, conv_x, conv_proj, norm_gain
):
    tokens, chans = x_stream.shape
    heads = dt_raw.shape[1]
    head_pos = lax.axis_index("head")
    ctx_pos = lax.axis_index("ctx")
    count = lax.axis_size("ctx")
    flag = jnp.stack([head_pos >> 1 & 1, ctx_pos, head_pos & 1]).astype(jnp.int32)

    proj_t = state_proj.T
    far_raw = swapped(proj_t, "head", 2)
    near_raw = swapped(proj_t, "head", 1)
    ends = tails(x_stream, proj_t, conv_proj)
    halo = rotated(ends, "ctx", 1)
    run, whole, step, totals, skip = decays(dt_raw.T, dt_bias, a_log, skip_d, chans)

    def conv(part, *needs):
        return chan_conv(flag, x_stream, conv_x, run, step, halo, part, 4, needs)

    x3, v3, mark = conv(3)
    halo_far = swapped(halo, "head", 2)
    halo_near = swapped(halo, "head", 1)
    x2, v2, mark = conv(2, halo, mark)
    x1, v1, mark = conv(1, mark)
    far_raw, halo_far, mark = lax.optimization_barrier((far_raw, halo_far, mark))
    cross_raw = swapped(far_raw, "head", 1)
    halo_cross = swapped(halo_far, "head", 1)
    x0, v0, mark = conv(0, far_raw, halo_far, mark)
    cross_raw, mark = lax.optimization_barrier((cross_raw, mark))
    raws = (proj_t, near_raw, far_raw, cross_raw)
    halos = (halo, halo_near, halo_far, halo_cross)
    b_t = proj_conv(flag, raws, halos, 0)
    entering, message = states((v0, v1, v2, v3), b_t, totals)
    c_t = proj_conv(flag, raws, halos, 1, (message,))

    locs = []

    def piece(at, *needs):
        x_conv = (x0, x1, x2, x3)[at]
        locs.append(
            local(x_conv, b_t, c_t, entering, run, step, skip, at, 4, 0, needs)
        )
        return locs[-1]

    one = opposed(message, 1)
    gate, fall = gates(gate_z, whole, (message, c_t))
    pair = merge(flag, message, one, 1, count, (fall,))
    two = opposed(pair, 2)
    piece(0, pair)
    last = piece(1, pair, locs[0])
    quad = merge(flag, pair, two, 2, count, (last,))
    four = opposed(quad, 4)
    piece(2, quad)
    piece(3, quad)
    msgs = (one, two, four)

    width = HEADS // GROUPS * (chans // heads)
    gated, squares = carry(flag, locs, gate, fall, c_t, msgs, count)
    squares = (squares + swapped(squares, "head", 1)) + (
        swapped(squares, "head", 2) + swapped(squares, "head", 3)
    )
    return norm(gated, squares, norm_gain[None, :], width)


def solution(mesh):
    return jax.shard_map(
        on_device,
        mesh=mesh,
        in_specs=(
            P("ctx", "head"),
            P("ctx", "head"),
            P("ctx", "head"),
            P("ctx", "head"),
            P("head"),
            P("head"),
            P("head"),
            P(None, "head"),
            P(None, "head"),
            P("head"),
        ),
        out_specs=P("ctx", "head"),
        check_vma=False,
    )
```
